1024 devices in a mesh: tm: 128 (over z_lo, y, x), head: 8 (over z_hi, core).
Axes of the slice: x: 4, y: 4, z: 32 (z_hi: 4, z_lo: 8; z = z_hi * 8 + z_lo), core: 2. Of those that a mesh axis runs over, the one named last changes fastest.
Arguments:
- query_rows: bfloat16 [32768, 4096], P('tm', 'head'), may hold values from -6 to 6
- key_rows: bfloat16 [32768, 4096], P('tm', 'head'), may hold values from -6 to 6
- value_rows: bfloat16 [32768, 4096], P('tm', 'head'), may hold values from -12 to 12
- frame_counts: int32 [128], replicated, may hold values from 1 to 4, 384 in all
- history: bfloat16 [256, 4096], P('tm', 'head'), may hold values from -3 to 3
- offsets: int32 [128, 128], P('tm'), may hold values from 0 to 127, each once within a row
- cotangent: bfloat16 [65536, 2048], P('tm'), may hold values from -0.09375 to 0.09375
Outputs:
- attended: bfloat16 [32768, 4096], P('tm', 'head')
- disc_grad: float32 [2048, 4096], P('tm', 'head')
The draws below stay inside these ranges and needn't reach their ends.
Inputs may be any that keep to these rules, and one draw needn't show every extreme that they name: Each row of offsets names every number below 128 once.
All inputs are finite; a program needn't handle non-finite values.
Results may differ from the reference program's by a relative error of at most 0.0049.
Values may be sent and summed in bfloat16 or wider, within the bound.
A program may use at most 32 MiB of HBM per device.

```python
import math
import jax
import jax.numpy as jnp
import numpy as np
from jax import lax

H = 32
HD = 128
D = 4096
FRAMES = 4
TPF = 64
TOK_DEV = 256
WINB = 4
TILE = 2
CLIP = 128
CLIP_TOK = 256
DH = 2048
TOKENS = 32768
HIST = 256
ROWS_ALL = 65536
N_TM = 128


def draw_query_rows(key, part):
    sub_key = jax.random.fold_in(key, 11)
    values_raw = jnp.clip(jax.random.normal(sub_key, (TOKENS, H * HD), jnp.float32), -6.0, 6.0)
    return values_raw.astype(jnp.bfloat16)


def draw_key_rows(key, part):
    sub_key = jax.random.fold_in(key, 12)
    values_raw = jnp.clip(jax.random.normal(sub_key, (TOKENS, H * HD), jnp.float32), -6.0, 6.0)
    return values_raw.astype(jnp.bfloat16)


def spiked(entries, key, source, target, parts, factor):
    owner, partner = [(jnp.arange(entries.shape[dim]) // (entries.shape[dim] // parts)).reshape([-1 if axis == dim else 1 for axis in range(entries.ndim)]) for dim in (source, target)]
    chosen = jax.random.permutation(key, parts)[partner]
    strong = (owner == chosen) | (owner == (partner + parts // 2) % parts)
    return jnp.where(strong, factor * entries, entries)


def block_levels(stream_key, shape, pieces, least, top_value):
    def one(position, parts):
        heights = jax.random.uniform(jax.random.fold_in(jax.random.fold_in(stream_key, 6), position), (parts,), jnp.float32, least / len(pieces), top_value / len(pieces))
        return jnp.repeat(jnp.exp(heights), shape[position] // parts).reshape((-1,) + (1,) * (len(shape) - position - 1))

    factor_of = one(*pieces[0])
    for cut in pieces[1:]:
        factor_of = factor_of * one(*cut)
    return factor_of


def split_up(amount, total, reach, skew):
    weights = [(1 << 20) // math.isqrt(rank ** skew) + 1 for rank in range(2, amount + 1)]
    spare, counts = total - reach - (amount - 1), [1] * (amount - 1)
    while spare > 0:
        candidates = [i for i in range(amount - 1) if counts[i] < reach]
        whole, budget = sum([weights[i] for i in candidates]), spare
        for i in candidates:
            extra = min(reach - counts[i], max(1, budget * weights[i] // whole), spare)
            counts[i] = counts[i] + extra
            spare = spare - extra
    return np.array([reach] + counts)


def ragged(stream_key, number_of, total, limit, skew):
    if number_of == 2:
        one = jax.random.randint(stream_key, (), max(1, total - limit), min(limit, total - 1) + 1)
        return jnp.stack([one, total - one])
    tallies = jnp.asarray(split_up(number_of, total, limit, skew), jnp.int32)
    pairs = (number_of - 1) // 2
    donor, sink = tallies[1:1 + 2 * pairs:2], tallies[2:2 + 2 * pairs:2]
    slack = jnp.minimum(donor - 1, limit - sink)
    passed = jax.random.randint(jax.random.fold_in(stream_key, 1), (pairs,), 0, 1 << 20) % (slack + 1)
    tallies = tallies.at[1:1 + 2 * pairs:2].set(donor - passed).at[2:2 + 2 * pairs:2].set(sink + passed)
    return tallies[jax.random.permutation(jax.random.fold_in(stream_key, 2), number_of)]


def centred(rng, shape, scale, bound, split=(), kind=jnp.bfloat16):
    result = jax.random.normal(rng, shape, jnp.float32) * scale
    if len(split) > 0:
        result = block_levels(rng, shape, split, -0.22, 0.18) * result
    return jnp.clip(result, min=-bound, max=bound).astype(kind)


def noise_with(rng, extent, width, most, shards, heavy, kind=jnp.bfloat16):
    values = width * jax.random.normal(rng, extent, jnp.float32)
    if shards:
        values = values * block_levels(rng, extent, shards, -0.22, 0.18)
    return jnp.clip(spiked(values, jax.random.fold_in(rng, 3), *heavy), -most, most).astype(kind)


def setup_inputs(seed: int = 0) -> dict:
    arg_keys = jax.random.split(jax.random.key(seed), 8)
    query_rows = draw_query_rows(jax.random.fold_in(arg_keys[7], 71), 0)
    key_rows = draw_key_rows(jax.random.fold_in(arg_keys[7], 71), 0)
    value_rows = centred(arg_keys[2], (TOKENS, D), 2.0, 12.0, ((0, 128), (1, 8)))
    frame_counts = ragged(arg_keys[3], N_TM, 3 * N_TM, FRAMES, 1).astype(jnp.int32)
    history = centred(arg_keys[4], (HIST, D), 0.5, 3.0, ((0, 128), (1, 8)))
    offsets = jax.vmap(lambda own: jax.random.permutation(own, N_TM))(jax.random.split(arg_keys[5], N_TM)).reshape((N_TM, CLIP)).astype(jnp.int32)
    cotangent = noise_with(arg_keys[6], (ROWS_ALL, DH), ROWS_ALL ** -0.5, 0.09375, ((0, 128),), (0, 1, 128, 5.5))
    return dict(query_rows=query_rows, key_rows=key_rows, value_rows=value_rows, frame_counts=frame_counts, history=history, offsets=offsets, cotangent=cotangent)


def reference(query_rows, key_rows, value_rows, frame_counts, history, offsets, cotangent):
    score_scale = 1.0 / math.sqrt(HD)
    query_blocks = query_rows.reshape(N_TM, TOK_DEV, H, HD)
    key_blocks = jnp.concatenate([jnp.zeros((WINB - 1, TOK_DEV, H, HD), key_rows.dtype), key_rows.reshape(N_TM, TOK_DEV, H, HD)], axis=0)
    value_blocks = jnp.concatenate([jnp.zeros((WINB - 1, TOK_DEV, H, HD), value_rows.dtype), value_rows.reshape(N_TM, TOK_DEV, H, HD)], axis=0)
    frame_index = jnp.arange(TOK_DEV, dtype=jnp.int32) // TPF
    kept_blocks = frame_index[None, :] < frame_counts[:, None]
    kept_padded = jnp.concatenate([jnp.zeros((WINB - 1, TOK_DEV), dtype=bool), kept_blocks], axis=0)

    def one_block(block_index):
        key_window = lax.dynamic_slice_in_dim(key_blocks, block_index, WINB, 0).reshape(WINB * TOK_DEV, H, HD)
        value_window = lax.dynamic_slice_in_dim(value_blocks, block_index, WINB, 0).reshape(WINB * TOK_DEV, H, HD)
        kept_window = lax.dynamic_slice_in_dim(kept_padded, block_index, WINB, 0).reshape(WINB * TOK_DEV)
        query_block = query_blocks[block_index]
        scores = jnp.einsum('qhd,khd->hqk', query_block.astype(jnp.float32), key_window.astype(jnp.float32)) * score_scale
        scores = jnp.where(kept_window[None, None, :], scores, -jnp.inf)
        row_max = lax.optimization_barrier(jnp.max(scores, axis=-1, keepdims=True))
        weights = jnp.exp(scores - row_max)
        probs = (weights / lax.optimization_barrier(jnp.sum(weights, axis=-1, keepdims=True))).astype(jnp.bfloat16)
        mixed = jnp.einsum('hqk,khd->qhd', probs.astype(jnp.float32), value_window.astype(jnp.float32))
        return mixed.astype(jnp.bfloat16).reshape(TOK_DEV, H * HD)
    attended = lax.map(one_block, jnp.arange(N_TM, dtype=jnp.int32)).reshape(TOKENS, H * HD)
    owners = jnp.arange(N_TM, dtype=jnp.int32)
    source_tile = (owners[:, None] - offsets) % N_TM
    source_row = (source_tile[:, :, None] * TILE + jnp.arange(TILE, dtype=jnp.int32)[None, None, :]).reshape(N_TM, CLIP_TOK)
    clip_hist = history[source_row]
    disc_clip = jnp.concatenate([clip_hist, attended.reshape(N_TM, TOK_DEV, H * HD)], axis=1).reshape(ROWS_ALL, H * HD)
    disc_grad = jnp.dot(cotangent.T, disc_clip, preferred_element_type=jnp.float32)
    return (attended, disc_grad)
```

```python
import math

import jax
import jax.numpy as jnp
from jax import lax
from jax.experimental import pallas as pl
from jax.experimental.pallas import tpu as pltpu
from jax.sharding import PartitionSpec as P

HD = 128
TPF = 64
WINB = 4
NX = 4
NY = 4
MESH = pl.DeviceIdType.MESH
F32 = jnp.float32
BF16 = jnp.bfloat16


def remote(src, dst, send, recv, target):
    return pltpu.make_async_remote_copy(
        src_ref=src,
        dst_ref=dst,
        send_sem=send,
        recv_sem=recv,
        device_id={"tm": target},
        device_id_type=MESH,
    )


def make_kernel(blocks, tok, feat, tiles, outs):
    nz = blocks // (NX * NY)
    half = feat // 2
    halves = (slice(0, half), slice(half, feat))
    heads = feat // HD
    rows = outs // blocks
    plane = outs // NX
    scale = 1.0 / math.sqrt(HD)

    def kernel(
        counts, query_hbm, key_hbm, value_hbm, history, offsets, cot_hbm,
        attended_ref, grad_ref,
        query, keys, values, cot, cot_t, clip, hist_all, hist_f32,
        send1, recv1, own1, send2, recv2, own2, send3, recv3, own3,
        local_sem, kv_send, kv_recv, ag_send, ag_recv,
        send1_sem, recv1_sem, send2_sem, recv2_sem, send3_sem, recv3_sem,
    ):
        me = lax.axis_index("tm")
        x = lax.rem(me, NX)
        y = lax.rem(me // NX, NY)
        z = me // (NX * NY)

        def at_x(k):
            return me - x + lax.rem(x + k, NX)

        def at_y(k):
            return me + (lax.rem(y + k, NY) - y) * NX

        def at_z(k):
            return me + (lax.rem(z + k, nz) - z) * (NX * NY)

        peers = [at_x(k) for k in range(1, NX)]
        peers += [at_y(k) for k in range(1, NY)]
        peers += [at_z(k) for k in range(1, nz)]

        local = [
            pltpu.make_async_copy(cot_hbm, cot, local_sem.at[0]),
            pltpu.make_async_copy(query_hbm, query, local_sem.at[1]),
            pltpu.make_async_copy(key_hbm, keys.at[WINB - 1], local_sem.at[2]),
            pltpu.make_async_copy(value_hbm, values.at[WINB - 1], local_sem.at[3]),
            pltpu.make_async_copy(history, hist_all.at[me], local_sem.at[4]),
        ]
        for copy in local:
            copy.start()

        barrier = pltpu.get_barrier_semaphore()
        for peer in peers:
            pl.semaphore_signal(barrier, inc=1, device_id={"tm": peer}, device_id_type=MESH)
        for distance in range(1, WINB):
            @pl.when(me >= distance)
            def _():
                pl.semaphore_signal(
                    barrier, inc=1, device_id={"tm": me - distance}, device_id_type=MESH
                )

            @pl.when(me + distance < blocks)
            def _():
                pl.semaphore_signal(
                    barrier, inc=1, device_id={"tm": me + distance}, device_id_type=MESH
                )
        around = jnp.minimum(me, WINB - 1) + jnp.minimum(blocks - 1 - me, WINB - 1)
        pl.semaphore_wait(barrier, len(peers) + around)

        kv = [[], []]
        for part in range(2):
            for distance in range(1, WINB):
                target = lax.rem(me + distance, blocks)
                for which, (src, dst) in enumerate(((key_hbm, keys), (value_hbm, values))):
                    i = (part * (WINB - 1) + distance - 1) * 2 + which
                    copy = remote(
                        src.at[:, halves[part]],
                        dst.at[WINB - 1 - distance, :, halves[part]],
                        kv_send.at[i],
                        kv_recv.at[i],
                        target,
                    )
                    kv[part].append((distance, copy))

        def start_kv(part):
            for distance, copy in kv[part]:
                @pl.when(me + distance < blocks)
                def _():
                    copy.start()

        def wait_kv(part):
            for distance, copy in kv[part]:
                @pl.when(me >= distance)
                def _():
                    copy.wait_recv()

        def gather(first, width, slot, targets):
            block = hist_all.at[pl.ds(first, width)]
            copies = []
            for i, target in enumerate(targets):
                copies.append(
                    remote(block, block, ag_send.at[slot + i], ag_recv.at[slot + i], target)
                )
            return copies

        gather_x = gather(me, 1, 0, [at_x(k) for k in range(1, NX)])
        gather_y = gather(me - x, NX, 3, [at_y(k) for k in range(1, NY)])
        gather_z = gather(z * NX * NY, NX * NY, 6, [at_z(k) for k in range(1, nz)])

        local[4].wait()
        for copy in gather_x:
            copy.start()
        start_kv(0)
        start_kv(1)

        for distance in range(1, WINB):
            @pl.when(me < distance)
            def _():
                keys[WINB - 1 - distance] = jnp.zeros((tok, feat), BF16)
                values[WINB - 1 - distance] = jnp.zeros((tok, feat), BF16)

        local[0].wait()

        def turn(c, _):
            block = cot[:, pl.ds(pl.multiple_of(c * 128, 128), 128)].T
            for e in range(128 // (NX * rows)):
                zy = c * (128 // (NX * rows)) + e
                for to_x in range(NX):
                    first = (e * NX + to_x) * rows
                    cot_t[to_x, lax.rem(zy, NY), zy // NY] = block[first : first + rows]
            return 0

        lax.fori_loop(0, outs // 256, turn, 0)
        for copy in gather_x:
            copy.wait_recv()
        for copy in gather_y:
            copy.start()
        lax.fori_loop(outs // 256, outs // 128, turn, 0)
        for copy in gather_y:
            copy.wait_recv()
        for copy in gather_z:
            copy.start()

        kept = []
        frame = lax.broadcasted_iota(jnp.int32, (1, tok), 1) // TPF
        for slot in range(WINB):
            source = me - (WINB - 1) + slot
            count = jnp.where(source >= 0, counts[jnp.maximum(source, 0)], 0)
            kept.append(frame < count)
        kept = jnp.concatenate(kept, axis=1)

        clip_rows = 2 * blocks
        tile = jnp.bitwise_and(me - offsets[...], blocks - 1).astype(F32).astype(BF16)
        spread = (
            lax.broadcasted_iota(jnp.int32, (blocks, clip_rows), 1) // tiles
            == lax.broadcasted_iota(jnp.int32, (blocks, clip_rows), 0)
        )
        spread = jnp.where(spread, 1.0, 0.0).astype(BF16)
        source_tile = jnp.dot(
            jnp.broadcast_to(tile, (16, blocks)), spread, preferred_element_type=F32
        )[0:1]
        hist_row = lax.broadcasted_iota(jnp.int32, (clip_rows, clip_rows), 0)
        clip_row = lax.broadcasted_iota(jnp.int32, (clip_rows, clip_rows), 1)
        chosen = (lax.rem(hist_row, blocks).astype(F32) == source_tile) & (
            hist_row // blocks == lax.rem(clip_row, tiles)
        )
        chosen = jnp.where(chosen, 1.0, 0.0).astype(BF16)

        for copy in gather_z:
            copy.wait_recv()
        hist_f32[...] = hist_all[...].astype(F32)
        pieces = []
        for t in range(tiles):
            line = [hist_f32[:, t * heads + c, :] for c in range(heads)]
            pieces.append(jnp.concatenate(line, axis=1))
        hist_rows = jnp.concatenate(pieces, axis=0).astype(BF16)
        clip[0:clip_rows] = lax.dot_general(
            chosen, hist_rows, (((0,), (0,)), ((), ())), preferred_element_type=F32
        ).astype(BF16)

        def attend(head):
            columns = slice(head * HD, (head + 1) * HD)
            key_head = keys[:, :, columns].reshape(WINB * tok, HD)
            value_head = values[:, :, columns].reshape(WINB * tok, HD)
            scores = lax.dot_general(
                query[:, columns], key_head, (((1,), (1,)), ((), ())), preferred_element_type=F32
            )
            scores = jnp.where(kept, scores * scale, -jnp.inf)
            weights = jnp.exp(scores - jnp.max(scores, axis=1, keepdims=True))
            probs = weights * (1.0 / jnp.sum(weights, axis=1, keepdims=True))
            mixed = jnp.dot(probs.astype(BF16), value_head, preferred_element_type=F32)
            clip[clip_rows : clip_rows + tok, columns] = mixed.astype(BF16)

        def product(part, to):
            left = cot_t[to] if part == 0 else cot_t[:, to]
            return jnp.dot(
                left.reshape(plane, clip_rows + tok),
                clip[:, halves[part]],
                preferred_element_type=F32,
            )

        place = (x, y)
        reach = (at_x, at_y)
        first_copies, second_copies, third_copies = [[], []], [[], []], [[], []]
        local[1].wait()
        local[2].wait()
        local[3].wait()
        for part in range(2):
            wait_kv(part)
            for head in range(part * heads // 2, (part + 1) * heads // 2):
                attend(head)
            for k in range(1, 4):
                send1[part, k - 1] = (
                    product(part, lax.rem(place[part] + k, 4)).astype(BF16).reshape(send1.shape[2:])
                )
                copy = remote(
                    send1.at[part, k - 1],
                    recv1.at[part, k - 1],
                    send1_sem.at[part, k - 1],
                    recv1_sem.at[part, k - 1],
                    reach[part](k),
                )
                copy.start()
                first_copies[part].append(copy)
            own1[part] = product(part, place[part]).reshape(own1.shape[1:])
        write_back = pltpu.make_async_copy(
            clip.at[clip_rows : clip_rows + tok], attended_ref, local_sem.at[5]
        )
        write_back.start()

        for part in range(2):
            for copy in first_copies[part]:
                copy.wait_recv()
            other = 1 - part

            def total1(to):
                total = own1[part, to]
                for k in range(3):
                    total += recv1[part, k, to].astype(F32)
                return total

            for k in range(1, 4):
                send2[part, k - 1] = total1(lax.rem(place[other] + k, 4)).astype(BF16)
                copy = remote(
                    send2.at[part, k - 1],
                    recv2.at[part, k - 1],
                    send2_sem.at[part, k - 1],
                    recv2_sem.at[part, k - 1],
                    reach[other](k),
                )
                copy.start()
                second_copies[part].append(copy)
            own2[part] = total1(place[other])

        for part in range(2):
            for copy in second_copies[part]:
                copy.wait_recv()
            total = own2[part]
            for k in range(3):
                total += recv2[part, k].astype(F32)
            own3[part] = total
            for k in range(1, nz):
                send3[part, k - 1] = own3[part, lax.rem(z + k, nz)].astype(BF16)
                copy = remote(
                    send3.at[part, k - 1],
                    recv3.at[part, k - 1],
                    send3_sem.at[part, k - 1],
                    recv3_sem.at[part, k - 1],
                    at_z(k),
                )
                copy.start()
                third_copies[part].append(copy)

        for part in range(2):
            for copy in third_copies[part]:
                copy.wait_recv()
            total = own3[part, z]
            for k in range(nz - 1):
                total += recv3[part, k].astype(F32)
            grad_ref[:, halves[part]] = total

        write_back.wait()
        for part in range(2):
            for distance, copy in kv[part]:
                @pl.when(me + distance < blocks)
                def _():
                    copy.wait_send()
            for copy in first_copies[part] + second_copies[part] + third_copies[part]:
                copy.wait_send()
        for copy in gather_x + gather_y + gather_z:
            copy.wait_send()

    return kernel


def body(query_rows, key_rows, value_rows, frame_counts, history, offsets, cotangent):
    tok, feat = query_rows.shape
    tiles = history.shape[0]
    outs = cotangent.shape[1]
    blocks = lax.axis_size("tm")
    nz = blocks // (NX * NY)
    rows = outs // blocks
    half = feat // 2
    clip_rows = tiles * blocks
    total_rows = clip_rows + tok
    lines = tiles * feat // 128
    dma = pltpu.SemaphoreType.DMA
    anywhere = pl.BlockSpec(memory_space=pl.ANY)
    vmem = pl.BlockSpec(memory_space=pltpu.VMEM)
    return pl.pallas_call(
        make_kernel(blocks, tok, feat, tiles, outs),
        out_shape=(
            jax.ShapeDtypeStruct((tok, feat), BF16),
            jax.ShapeDtypeStruct((rows, feat), F32),
        ),
        in_specs=[
            pl.BlockSpec(memory_space=pltpu.SMEM),
            anywhere,
            anywhere,
            anywhere,
            anywhere,
            vmem,
            anywhere,
        ],
        out_specs=(anywhere, vmem),
        scratch_shapes=[
            pltpu.VMEM((tok, feat), BF16),
            pltpu.VMEM((WINB, tok, feat), BF16),
            pltpu.VMEM((WINB, tok, feat), BF16),
            pltpu.VMEM((total_rows, outs), BF16),
            pltpu.VMEM((NX, NY, nz, rows, total_rows), BF16),
            pltpu.VMEM((total_rows, feat), BF16),
            pltpu.VMEM((blocks, lines, 128), BF16),
            pltpu.VMEM((blocks, lines, 128), F32),
            pltpu.VMEM((2, 3, 4, nz, rows, half), BF16),
            pltpu.VMEM((2, 3, 4, nz, rows, half), BF16),
            pltpu.VMEM((2, 4, nz, rows, half), F32),
            pltpu.VMEM((2, 3, nz, rows, half), BF16),
            pltpu.VMEM((2, 3, nz, rows, half), BF16),
            pltpu.VMEM((2, nz, rows, half), F32),
            pltpu.VMEM((2, nz - 1, rows, half), BF16),
            pltpu.VMEM((2, nz - 1, rows, half), BF16),
            pltpu.VMEM((2, nz, rows, half), F32),
            dma((6,)),
            dma((12,)),
            dma((12,)),
            dma((6 + nz - 1,)),
            dma((6 + nz - 1,)),
            dma((2, 3)),
            dma((2, 3)),
            dma((2, 3)),
            dma((2, 3)),
            dma((2, nz - 1)),
            dma((2, nz - 1)),
        ],
        compiler_params=pltpu.CompilerParams(
            collective_id=0, has_side_effects=True, vmem_limit_bytes=48 << 20
        ),
    )(
        frame_counts,
        query_rows,
        key_rows,
        value_rows,
        history.reshape(lines, 128),
        offsets,
        cotangent,
    )


def solution(mesh):
    in_specs = (
        P("tm", "head"),
        P("tm", "head"),
        P("tm", "head"),
        P(),
        P("tm", "head"),
        P("tm", None),
        P("tm", None),
    )
    out_specs = (P("tm", "head"), P("tm", "head"))
    return jax.shard_map(body, mesh=mesh, in_specs=in_specs, out_specs=out_specs, check_vma=False)
```

```python
import math

import jax
import jax.numpy as jnp
from jax import lax
from jax.experimental import pallas as pl
from jax.experimental.pallas import tpu as pltpu
from jax.sharding import PartitionSpec as P

HD = 128
TPF = 64
WINB = 4
NX = 4
NY = 4
STREAMS = (0, 1)
MESH = pl.DeviceIdType.MESH
F32 = jnp.float32
BF16 = jnp.bfloat16


def remote(src, dst, send, recv, target):
    return pltpu.make_async_remote_copy(
        src_ref=src,
        dst_ref=dst,
        send_sem=send,
        recv_sem=recv,
        device_id={"tm": target},
        device_id_type=MESH,
    )


def make_kernel(blocks, tok, feat, tiles, outs, streams):
    nz = blocks // (NX * NY)
    half = feat // 2
    halves = (slice(0, half), slice(half, feat))
    heads = feat // HD
    rows = outs // blocks
    plane = outs // NX
    scale = 1.0 / math.sqrt(HD)

    def kernel(
        counts, query_hbm, key_hbm, value_hbm, history, offsets, cot_hbm,
        attended_ref, grad_ref,
        query, keys, values, mixed, cot, cot_t, clip, hist_all, hist_f32,
        local_sem, row_send, row_recv, kv_send, kv_recv, out_send, out_recv, ag_send, ag_recv,
        *stream_refs,
    ):
        me = lax.axis_index("tm")
        refs = [stream_refs[13 * i : 13 * (i + 1)] for i in range(len(streams))]
        x = lax.rem(me, NX)
        y = lax.rem(me // NX, NY)
        z = me // (NX * NY)

        def at_x(k):
            return me - x + lax.rem(x + k, NX)

        def at_y(k):
            return me + (lax.rem(y + k, NY) - y) * NX

        def at_z(k):
            return me + (lax.rem(z + k, nz) - z) * (NX * NY)

        has_before = me >= NX
        has_after = me + NX < blocks
        peers = [at_x(k) for k in range(1, NX)]
        peers += [at_y(k) for k in range(1, NY)]
        peers += [at_z(k) for k in range(1, nz)]

        def columns(head):
            return pl.ds(pl.multiple_of(head * HD, HD), HD)

        own_head = columns(x)
        last = WINB - 1
        local = [
            pltpu.make_async_copy(cot_hbm, cot, local_sem.at[0]),
            pltpu.make_async_copy(query_hbm.at[:, own_head], query.at[x], local_sem.at[1]),
            pltpu.make_async_copy(key_hbm.at[:, own_head], keys.at[last + x], local_sem.at[2]),
            pltpu.make_async_copy(value_hbm.at[:, own_head], values.at[last + x], local_sem.at[3]),
            pltpu.make_async_copy(
                history, hist_all.at[(y * NX + x) * nz + z], local_sem.at[4]
            ),
        ]
        for copy in local:
            copy.start()

        barrier = pltpu.get_barrier_semaphore()
        for peer in peers:
            pl.semaphore_signal(barrier, inc=1, device_id={"tm": peer}, device_id_type=MESH)
        @pl.when(has_before)
        def _():
            pl.semaphore_signal(
                barrier, inc=1, device_id={"tm": me - NX}, device_id_type=MESH
            )

        @pl.when(has_after)
        def _():
            pl.semaphore_signal(
                barrier, inc=1, device_id={"tm": me + NX}, device_id_type=MESH
            )

        around = has_before.astype(jnp.int32) + has_after.astype(jnp.int32)
        pl.semaphore_wait(barrier, len(peers) + around)

        swaps = []
        for which, (src, dst, first) in enumerate(
            ((key_hbm, keys, last), (value_hbm, values, last), (query_hbm, query, 0))
        ):
            swaps.append(
                [
                    remote(
                        src.at[:, columns(lax.rem(x + k, NX))],
                        dst.at[first + x],
                        kv_send.at[which * (NX - 1) + k - 1],
                        kv_recv.at[which * (NX - 1) + k - 1],
                        at_x(k),
                    )
                    for k in range(1, NX)
                ]
            )
        forward = [
            remote(
                ref.at[WINB : WINB + NX - 1],
                ref.at[0 : NX - 1],
                row_send.at[which],
                row_recv.at[which],
                lax.rem(me + NX, blocks),
            )
            for which, ref in enumerate((keys, values))
        ]

        def gather(first, width, slot, targets):
            block = hist_all.at[pl.ds(first, width)]
            copies = []
            for i, target in enumerate(targets):
                copies.append(
                    remote(block, block, ag_send.at[slot + i], ag_recv.at[slot + i], target)
                )
            return copies

        column = (y * NX + x) * nz
        gather_z = gather(column + z, 1, 6, [at_z(k) for k in range(1, nz)])
        gather_x = gather(column, nz, 0, [at_x(k) for k in range(1, NX)])
        gather_y = gather(y * NX * nz, NX * nz, 3, [at_y(k) for k in range(1, NY)])

        def start(copies):
            for copy in copies:
                copy.start()

        def arrive(copies):
            for copy in copies:
                copy.wait_recv()

        local[4].wait()
        start(gather_z)
        start(swaps[0])
        start(swaps[1])

        @pl.when(jnp.logical_not(has_before))
        def _():
            keys[0 : NX - 1] = jnp.zeros((NX - 1, tok, HD), BF16)
            values[0 : NX - 1] = jnp.zeros((NX - 1, tok, HD), BF16)

        def turn(c, _):
            block = cot[:, pl.ds(pl.multiple_of(c * 128, 128), 128)].T
            for e in range(128 // (NX * rows)):
                zy = c * (128 // (NX * rows)) + e
                to_y = lax.rem(lax.rem(zy, NY) + NY - y, NY)
                to_z = lax.rem(zy // NY + nz - z, nz)
                for i in range(NX):
                    first = (e * NX + i) * rows
                    cot_t[lax.rem(i + NX - x, NX), to_y, to_z] = block[first : first + rows]
            return 0

        local[0].wait()
        turns = outs // 128
        lax.fori_loop(0, turns // 2, turn, 0)
        local[2].wait()
        arrive(swaps[0])
        pl.when(has_after)(forward[0].start)
        start(swaps[2])
        arrive(gather_z)
        start(gather_x)
        local[3].wait()
        arrive(swaps[1])
        pl.when(has_after)(forward[1].start)
        lax.fori_loop(turns // 2, turns, turn, 0)

        kept = []
        frame = lax.broadcasted_iota(jnp.int32, (1, tok), 1) // TPF
        for slot in range(last + NX):
            source = me - x - last + slot
            count = jnp.where(source >= 0, counts[jnp.maximum(source, 0)], 0)
            kept.append(frame < count)

        clip_rows = tiles * blocks
        tile = jnp.bitwise_and(me - offsets[...], blocks - 1)
        tile = lax.rem(tile, NX * NY) * nz + tile // (NX * NY)
        spread = (
            lax.broadcasted_iota(jnp.int32, (blocks, clip_rows), 1) // tiles
            == lax.broadcasted_iota(jnp.int32, (blocks, clip_rows), 0)
        )
        spread = jnp.where(spread, 1.0, 0.0).astype(BF16)
        source_tile = jnp.dot(
            jnp.broadcast_to(tile.astype(F32).astype(BF16), (16, blocks)),
            spread,
            preferred_element_type=F32,
        )[0:1]
        hist_row = lax.broadcasted_iota(jnp.int32, (clip_rows, clip_rows), 0)
        clip_row = lax.broadcasted_iota(jnp.int32, (clip_rows, clip_rows), 1)
        chosen = (lax.rem(hist_row, blocks).astype(F32) == source_tile) & (
            hist_row // blocks == lax.rem(clip_row, tiles)
        )
        chosen = jnp.where(chosen, 1.0, 0.0).astype(BF16)

        arrive(gather_x)
        start(gather_y)

        def attend(i):
            key_head = keys[i : i + WINB].reshape(WINB * tok, HD)
            value_head = values[i : i + WINB].reshape(WINB * tok, HD)
            scores = lax.dot_general(
                query[i], key_head, (((1,), (1,)), ((), ())), preferred_element_type=F32
            )
            seen = jnp.concatenate(kept[i : i + WINB], axis=1)
            scores = jnp.where(seen, scores * scale, -jnp.inf)
            weights = jnp.exp(scores - jnp.max(scores, axis=1, keepdims=True))
            probs = weights * (1.0 / jnp.sum(weights, axis=1, keepdims=True))
            mixed[i] = jnp.dot(
                probs.astype(BF16), value_head, preferred_element_type=F32
            ).astype(BF16)

        attended = clip.at[clip_rows : clip_rows + tok]
        backs = [
            remote(
                mixed.at[i],
                attended.at[:, own_head],
                out_send.at[i],
                out_recv.at[x],
                me - x + i,
            )
            for i in range(NX)
        ]
        stay = pltpu.make_async_copy(mixed.at[x], attended.at[:, own_head], local_sem.at[1])
        local[1].wait()
        arrive(swaps[2])
        for i in range(NX - 1, -1, -1):
            if i == NX - 2:
                pl.when(has_before)(forward[0].wait_recv)
                pl.when(has_before)(forward[1].wait_recv)
            attend(i)
            pl.when(x != i)(backs[i].start)
        stay.start()

        arrive(gather_y)
        hist_f32[...] = hist_all[...].astype(F32)
        pieces = []
        for t in range(tiles):
            line = [hist_f32[:, t * heads + c, :] for c in range(heads)]
            pieces.append(jnp.concatenate(line, axis=1))
        hist_rows = jnp.concatenate(pieces, axis=0).astype(BF16)
        clip[0:clip_rows] = lax.dot_general(
            chosen, hist_rows, (((0,), (0,)), ((), ())), preferred_element_type=F32
        ).astype(BF16)
        for k in range(1, NX):
            other = lax.rem(x + k, NX)
            remote(
                mixed.at[0], attended.at[:, columns(other)], out_send.at[0], out_recv.at[other], at_x(k)
            ).wait_recv()
        stay.wait()

        reach = (at_x, at_y)
        sends = []

        def send(src, dst, send_sem, recv_sem, target):
            copy = remote(src, dst, send_sem, recv_sem, target)
            copy.start()
            sends.append(copy)
            return copy

        stage1 = [[[None] * 4 for _ in range(3)] for _ in streams]
        stage2 = [[None] * 3 for _ in streams]
        stage3 = [[None] * (nz - 1) for _ in streams]

        def product(i, k):
            s1, r1, own1, s1_sem, r1_sem = refs[i][0], refs[i][1], refs[i][2], refs[i][7], refs[i][8]
            left = cot_t[k] if streams[i] == 0 else cot_t[:, k]
            block = jnp.dot(
                left.reshape(outs // 4, clip_rows + tok),
                clip[:, halves[i]],
                preferred_element_type=F32,
            ).reshape(4, nz, rows, half)
            if k == 0:
                own1[...] = block
                return
            s1[k - 1] = block.astype(BF16)
            for j in (1, 2, 3, 0):
                stage1[i][k - 1][j] = send(
                    s1.at[k - 1, j],
                    r1.at[k - 1, j],
                    s1_sem.at[k - 1, j],
                    r1_sem.at[k - 1, j],
                    reach[streams[i]](k),
                )

        def second(i, j):
            r1, own1, s2, r2 = refs[i][1], refs[i][2], refs[i][3], refs[i][4]
            for k in range(3):
                stage1[i][k][j].wait_recv()
            total = own1[j]
            for k in range(3):
                total += r1[k, j].astype(F32)
            if j == 0:
                own1[0] = total
                return
            s2[j - 1] = total.astype(BF16)
            stage2[i][j - 1] = send(
                s2.at[j - 1],
                r2.at[j - 1],
                refs[i][9].at[j - 1],
                refs[i][10].at[j - 1],
                reach[1 - streams[i]](j),
            )

        def third(i):
            own1, r2, s3, r3 = refs[i][2], refs[i][4], refs[i][5], refs[i][6]
            arrive(stage2[i])
            total = own1[0]
            for k in range(3):
                total += r2[k].astype(F32)
            own1[1, 0] = total[0]
            s3[...] = total[1:].astype(BF16)
            for k in range(1, nz):
                stage3[i][k - 1] = send(
                    s3.at[k - 1],
                    r3.at[k - 1],
                    refs[i][11].at[k - 1],
                    refs[i][12].at[k - 1],
                    at_z(k),
                )

        def finish(i):
            arrive(stage3[i])
            total = refs[i][2][1, 0]
            for k in range(nz - 1):
                total += refs[i][6][k].astype(F32)
            grad_ref[:, halves[i]] = total

        every = range(len(streams))
        for k in (1, 2, 3, 0):
            for i in every:
                product(i, k)
        write_back = pltpu.make_async_copy(
            attended, attended_ref, local_sem.at[5]
        )
        write_back.start()
        for j in (1, 2, 3, 0):
            for i in every:
                second(i, j)
        for i in every:
            third(i)
        for i in every:
            finish(i)

        write_back.wait()
        for copy in forward:
            pl.when(has_after)(copy.wait_send)
        for i in range(NX):
            pl.when(x != i)(backs[i].wait_send)
        for copy in swaps[0] + swaps[1] + swaps[2] + gather_x + gather_y + gather_z + sends:
            copy.wait_send()

    return kernel


def body(query_rows, key_rows, value_rows, frame_counts, history, offsets, cotangent):
    tok, feat = query_rows.shape
    tiles = history.shape[0]
    outs = cotangent.shape[1]
    blocks = lax.axis_size("tm")
    nz = blocks // (NX * NY)
    rows = outs // blocks
    half = feat // 2
    clip_rows = tiles * blocks
    total_rows = clip_rows + tok
    lines = tiles * feat // 128
    dma = pltpu.SemaphoreType.DMA
    anywhere = pl.BlockSpec(memory_space=pltpu.HBM)
    vmem = pl.BlockSpec(memory_space=pltpu.VMEM)
    streams = STREAMS
    width = half
    stream_scratch = []
    for _ in streams:
        stream_scratch += [
            pltpu.VMEM((3, 4, nz, rows, width), BF16),
            pltpu.VMEM((3, 4, nz, rows, width), BF16),
            pltpu.VMEM((4, nz, rows, width), F32),
            pltpu.VMEM((3, nz, rows, width), BF16),
            pltpu.VMEM((3, nz, rows, width), BF16),
            pltpu.VMEM((nz - 1, rows, width), BF16),
            pltpu.VMEM((nz - 1, rows, width), BF16),
            dma((3, 4)),
            dma((3, 4)),
            dma((3,)),
            dma((3,)),
            dma((nz - 1,)),
            dma((nz - 1,)),
        ]
    return pl.pallas_call(
        make_kernel(blocks, tok, feat, tiles, outs, streams),
        out_shape=(
            jax.ShapeDtypeStruct((tok, feat), BF16),
            jax.ShapeDtypeStruct((rows, feat), F32),
        ),
        in_specs=[
            pl.BlockSpec(memory_space=pltpu.SMEM),
            anywhere,
            anywhere,
            anywhere,
            anywhere,
            vmem,
            anywhere,
        ],
        out_specs=(anywhere, vmem),
        scratch_shapes=[
            pltpu.VMEM((NX, tok, HD), BF16),
            pltpu.VMEM((WINB - 1 + NX, tok, HD), BF16),
            pltpu.VMEM((WINB - 1 + NX, tok, HD), BF16),
            pltpu.VMEM((NX, tok, HD), BF16),
            pltpu.VMEM((total_rows, outs), BF16),
            pltpu.VMEM((NX, NY, nz, rows, total_rows), BF16),
            pltpu.VMEM((total_rows, feat), BF16),
            pltpu.VMEM((blocks, lines, 128), BF16),
            pltpu.VMEM((blocks, lines, 128), F32),
            dma((6,)),
            dma((2,)),
            dma((2,)),
            dma((9,)),
            dma((9,)),
            dma((NX,)),
            dma((NX,)),
            dma((6 + nz - 1,)),
            dma((6 + nz - 1,)),
        ]
        + stream_scratch,
        compiler_params=pltpu.CompilerParams(
            collective_id=0, has_side_effects=True, vmem_limit_bytes=60 << 20
        ),
    )(
        frame_counts,
        query_rows,
        key_rows,
        value_rows,
        history.reshape(lines, 128),
        offsets,
        cotangent,
    )


def solution(mesh):
    in_specs = (
        P("tm", "head"),
        P("tm", "head"),
        P("tm", "head"),
        P(),
        P("tm", "head"),
        P("tm", None),
        P("tm", None),
    )
    out_specs = (P("tm", "head"), P("tm", "head"))
    return jax.shard_map(body, mesh=mesh, in_specs=in_specs, out_specs=out_specs, check_vma=False)
```

```python
import math

import jax
import jax.numpy as jnp
from jax import lax
from jax.experimental import pallas as pl
from jax.experimental.pallas import tpu as pltpu
from jax.sharding import PartitionSpec as P

HD = 128
TPF = 64
WINB = 4
NX = 4
NY = 4
STREAMS = (0, 1)
MESH = pl.DeviceIdType.MESH
F32 = jnp.float32
BF16 = jnp.bfloat16


def remote(src, dst, send, recv, target):
    return pltpu.make_async_remote_copy(
        src_ref=src,
        dst_ref=dst,
        send_sem=send,
        recv_sem=recv,
        device_id={"tm": target},
        device_id_type=MESH,
    )


def make_kernel(blocks, tok, feat, tiles, outs, streams):
    nz = blocks // (NX * NY)
    half = feat // 2
    halves = (slice(0, half), slice(half, feat))
    heads = feat // HD
    rows = outs // blocks
    plane = outs // NX
    scale = 1.0 / math.sqrt(HD)

    def kernel(
        counts, query_hbm, key_hbm, value_hbm, history, offsets, cot_hbm,
        attended_ref, grad_ref,
        query, keys, values, mixed, cot, cot_t, clip, hist_all, hist_f32,
        local_sem, row_send, row_recv, ahead_send, ahead_recv, kv_send, kv_recv, out_send, out_recv, ag_send, ag_recv,
        *stream_refs,
    ):
        me = lax.axis_index("tm")
        refs = [stream_refs[18 * i : 18 * (i + 1)] for i in range(len(streams))]
        x = lax.rem(me, NX)
        y = lax.rem(me // NX, NY)
        z = me // (NX * NY)

        def at_x(k):
            return me - x + lax.rem(x + k, NX)

        def at_y(k):
            return me + (lax.rem(y + k, NY) - y) * NX

        def at_z(k):
            return me + (lax.rem(z + k, nz) - z) * (NX * NY)

        has_before = me >= NX
        has_after = me + NX < blocks
        peers = [at_x(k) for k in range(1, NX)]
        peers += [at_y(k) for k in range(1, NY)]
        peers += [at_z(k) for k in range(1, nz)]

        def columns(head):
            return pl.ds(pl.multiple_of(head * HD, HD), HD)

        own_head = columns(x)
        last = WINB - 1
        local = [
            pltpu.make_async_copy(cot_hbm, cot, local_sem.at[0]),
            pltpu.make_async_copy(query_hbm.at[:, own_head], query.at[x], local_sem.at[1]),
            pltpu.make_async_copy(key_hbm.at[:, own_head], keys.at[last + x], local_sem.at[2]),
            pltpu.make_async_copy(value_hbm.at[:, own_head], values.at[last + x], local_sem.at[3]),
        ]
        for copy in local:
            copy.start()

        barrier = pltpu.get_barrier_semaphore()
        for peer in peers:
            pl.semaphore_signal(barrier, inc=1, device_id={"tm": peer}, device_id_type=MESH)
        @pl.when(has_before)
        def _():
            for i in range(NX):
                pl.semaphore_signal(
                    barrier, inc=1, device_id={"tm": me - x - NX + i}, device_id_type=MESH
                )

        pl.semaphore_wait(barrier, len(peers) + jnp.where(has_after, NX, 0))

        swaps = []
        for which, (src, dst, first) in enumerate(
            ((key_hbm, keys, last), (value_hbm, values, last), (query_hbm, query, 0))
        ):
            swaps.append(
                [
                    remote(
                        src.at[:, columns(lax.rem(x + k, NX))],
                        dst.at[first + x],
                        kv_send.at[which * (NX - 1) + k - 1],
                        kv_recv.at[which * (NX - 1) + k - 1],
                        at_x(k),
                    )
                    for k in range(1, NX)
                ]
            )
        ahead = [
            remote(
                key_hbm.at[:, i * HD : (i + 1) * HD],
                keys.at[jnp.maximum(x - 1, 0)],
                ahead_send.at[i],
                ahead_recv.at[jnp.maximum(x - 1, 0)],
                lax.rem(me - x + NX + i, blocks),
            )
            for i in range(NX)
        ]
        sends_ahead = has_after & (x > 0)
        forward = remote(
            values.at[WINB : WINB + NX - 1],
            values.at[0 : NX - 1],
            row_send.at[0],
            row_recv.at[0],
            lax.rem(me + NX, blocks),
        )

        def arrive_ahead():
            for i in range(NX - 1):
                remote(
                    key_hbm.at[:, 0:HD],
                    keys.at[i],
                    ahead_send.at[i],
                    ahead_recv.at[i],
                    lax.rem(me + NX, blocks),
                ).wait_recv()

        def gather(first, width, slot, targets):
            block = hist_all.at[pl.ds(first, width)]
            copies = []
            for i, target in enumerate(targets):
                copies.append(
                    remote(block, block, ag_send.at[slot + i], ag_recv.at[slot + i], target)
                )
            return copies

        column = (y * NX + x) * nz
        gather_z = gather(column + z, 1, 6, [at_z(k) for k in range(1, nz)])
        gather_x = gather(column, nz, 0, [at_x(k) for k in range(1, NX)])
        gather_y = gather(y * NX * nz, NX * nz, 3, [at_y(k) for k in range(1, NY)])

        def start(copies):
            for copy in copies:
                copy.start()

        def arrive(copies):
            for copy in copies:
                copy.wait_recv()

        line = history[...].astype(F32)
        hist_all[column + z] = jnp.concatenate(
            [line[t : t + 1, c * 128 : (c + 1) * 128] for t in range(tiles) for c in range(heads)],
            axis=0,
        ).astype(BF16)
        start(gather_z)
        start(swaps[1])

        @pl.when(sends_ahead)
        def _():
            for copy in ahead:
                copy.start()

        start(swaps[0])
        start(swaps[2])

        @pl.when(jnp.logical_not(has_before))
        def _():
            keys[0 : NX - 1] = jnp.zeros((NX - 1, tok, HD), BF16)
            values[0 : NX - 1] = jnp.zeros((NX - 1, tok, HD), BF16)

        def turn(c, _):
            block = cot[:, pl.ds(pl.multiple_of(c * 128, 128), 128)].T
            for e in range(128 // (NX * rows)):
                zy = c * (128 // (NX * rows)) + e
                to_y = lax.rem(lax.rem(zy, NY) + NY - y, NY)
                to_z = lax.rem(zy // NY + nz - z, nz)
                for i in range(NX):
                    first = (e * NX + i) * rows
                    cot_t[lax.rem(i + NX - x, NX), to_y, to_z] = block[first : first + rows]
            return 0

        local[0].wait()
        turns = outs // 128
        lax.fori_loop(0, turns // 2, turn, 0)
        local[3].wait()
        arrive(swaps[1])
        pl.when(has_after)(forward.start)
        arrive(gather_z)
        start(gather_x)
        lax.fori_loop(turns // 2, turns, turn, 0)

        kept = []
        frame = lax.broadcasted_iota(jnp.int32, (1, tok), 1) // TPF
        for slot in range(last + NX):
            source = me - x - last + slot
            count = jnp.where(source >= 0, counts[jnp.maximum(source, 0)], 0)
            kept.append(frame < count)

        clip_rows = tiles * blocks
        tile = jnp.bitwise_and(me - offsets[...], blocks - 1)
        tile = lax.rem(tile, NX * NY) * nz + tile // (NX * NY)
        spread = (
            lax.broadcasted_iota(jnp.int32, (blocks, clip_rows), 1) // tiles
            == lax.broadcasted_iota(jnp.int32, (blocks, clip_rows), 0)
        )
        spread = jnp.where(spread, 1.0, 0.0).astype(BF16)
        source_tile = jnp.dot(
            jnp.broadcast_to(tile.astype(F32).astype(BF16), (16, blocks)),
            spread,
            preferred_element_type=F32,
        )[0:1]
        hist_row = lax.broadcasted_iota(jnp.int32, (clip_rows, clip_rows), 0)
        clip_row = lax.broadcasted_iota(jnp.int32, (clip_rows, clip_rows), 1)
        chosen = (lax.rem(hist_row, blocks).astype(F32) == source_tile) & (
            hist_row // blocks == lax.rem(clip_row, tiles)
        )
        chosen = jnp.where(chosen, 1.0, 0.0).astype(BF16)

        arrive(gather_x)
        start(gather_y)

        def attend(i):
            key_head = keys[i : i + WINB].reshape(WINB * tok, HD)
            value_head = values[i : i + WINB].reshape(WINB * tok, HD)
            scores = lax.dot_general(
                query[i], key_head, (((1,), (1,)), ((), ())), preferred_element_type=F32
            )
            seen = jnp.concatenate(kept[i : i + WINB], axis=1)
            scores = jnp.where(seen, scores * scale, -jnp.inf)
            weights = jnp.exp(scores - jnp.max(scores, axis=1, keepdims=True))
            probs = weights * (1.0 / jnp.sum(weights, axis=1, keepdims=True))
            mixed[i] = jnp.dot(
                probs.astype(BF16), value_head, preferred_element_type=F32
            ).astype(BF16)

        attended = clip.at[clip_rows : clip_rows + tok]
        backs = [
            remote(
                mixed.at[i],
                attended.at[:, own_head],
                out_send.at[i],
                out_recv.at[x],
                me - x + i,
            )
            for i in range(NX)
        ]
        stay = pltpu.make_async_copy(mixed.at[x], attended.at[:, own_head], local_sem.at[1])
        local[1].wait()
        local[2].wait()
        arrive(swaps[0])
        arrive(swaps[2])
        for i in range(NX - 1, -1, -1):
            if i == NX - 2:
                pl.when(has_before)(arrive_ahead)
                pl.when(has_before)(forward.wait_recv)
            attend(i)
            pl.when(x != i)(backs[i].start)
        stay.start()

        arrive(gather_y)
        hist_f32[...] = hist_all[...].astype(F32)
        pieces = []
        for t in range(tiles):
            line = [hist_f32[:, t * heads + c, :] for c in range(heads)]
            pieces.append(jnp.concatenate(line, axis=1))
        hist_rows = jnp.concatenate(pieces, axis=0).astype(BF16)
        clip[0:clip_rows] = lax.dot_general(
            chosen, hist_rows, (((0,), (0,)), ((), ())), preferred_element_type=F32
        ).astype(BF16)
        for k in range(1, NX):
            other = lax.rem(x + k, NX)
            remote(
                mixed.at[0], attended.at[:, columns(other)], out_send.at[0], out_recv.at[other], at_x(k)
            ).wait_recv()
        stay.wait()

        reach = (at_x, at_y)
        sends = []

        def send(src, dst, send_sem, recv_sem, target):
            copy = remote(src, dst, send_sem, recv_sem, target)
            copy.start()
            sends.append(copy)
            return copy

        stage2 = [[None] * 3 for _ in streams]
        stage3 = [[None] * (nz - 1) for _ in streams]
        relays = [[None] * 4 for _ in streams]
        direct = [[[None] * 4 for _ in range(2)] for _ in streams]

        def dot1(i, k):
            left = cot_t[k] if streams[i] == 0 else cot_t[:, k]
            return jnp.dot(
                left.reshape(outs // 4, clip_rows + tok),
                clip[:, halves[i]],
                preferred_element_type=F32,
            ).reshape(4, nz, rows, half)

        up, down = (1, 3), (2, 0)

        def opposite(i):
            s0, r0 = refs[i][13], refs[i][14]
            s0[...] = dot1(i, 2).astype(BF16)
            for j in (1, 2, 3, 0):
                relays[i][j] = send(
                    s0.at[j],
                    r0.at[j],
                    refs[i][15].at[j],
                    refs[i][16].at[j],
                    reach[streams[i]](1 if j in up else 3),
                )

        def pass1(i, side, js):
            s1, r1, s1_sem, r1_sem = refs[i][0], refs[i][1], refs[i][7], refs[i][8]
            for j in js:
                direct[i][side][j] = send(
                    s1.at[side, j],
                    r1.at[side, j],
                    s1_sem.at[side, j],
                    r1_sem.at[side, j],
                    reach[streams[i]](1 if side == 0 else 3),
                )

        def beside(i, side):
            block = dot1(i, 1 if side == 0 else 3)
            through = up if side == 0 else down
            for j in range(4):
                if j in through:
                    refs[i][17][j] = block[j]
                else:
                    refs[i][0][side, j] = block[j].astype(BF16)
            pass1(i, side, down if side == 0 else up)

        def through1(i, side):
            for j in up if side == 0 else down:
                relays[i][j].wait_recv()
                total = refs[i][17][j] + refs[i][14][j].astype(F32)
                refs[i][0][side, j] = total.astype(BF16)
                pass1(i, side, (j,))

        def second(i, j):
            r1, own1, s2, r2 = refs[i][1], refs[i][2], refs[i][3], refs[i][4]
            direct[i][0][j].wait_recv()
            direct[i][1][j].wait_recv()
            total = own1[j] + r1[0, j].astype(F32) + r1[1, j].astype(F32)
            if j == 0:
                own1[0] = total
                return
            s2[j - 1] = total.astype(BF16)
            stage2[i][j - 1] = send(
                s2.at[j - 1],
                r2.at[j - 1],
                refs[i][9].at[j - 1],
                refs[i][10].at[j - 1],
                reach[1 - streams[i]](j),
            )

        def third(i):
            own1, r2, s3, r3 = refs[i][2], refs[i][4], refs[i][5], refs[i][6]
            arrive(stage2[i])
            total = own1[0]
            for k in range(3):
                total += r2[k].astype(F32)
            own1[1, 0] = total[0]
            s3[...] = total[1:].astype(BF16)
            for k in range(1, nz):
                stage3[i][k - 1] = send(
                    s3.at[k - 1],
                    r3.at[k - 1],
                    refs[i][11].at[k - 1],
                    refs[i][12].at[k - 1],
                    at_z(k),
                )

        def finish(i):
            arrive(stage3[i])
            total = refs[i][2][1, 0]
            for k in range(nz - 1):
                total += refs[i][6][k].astype(F32)
            grad_ref[:, halves[i]] = total

        every = range(len(streams))
        for i in every:
            opposite(i)
        for side in range(2):
            for i in every:
                beside(i, side)
        for i in every:
            refs[i][2][...] = dot1(i, 0)
        for side in range(2):
            for i in every:
                through1(i, side)
        write_back = pltpu.make_async_copy(
            attended, attended_ref, local_sem.at[5]
        )
        write_back.start()
        for j in (1, 2, 3, 0):
            for i in every:
                second(i, j)
        for i in every:
            third(i)
        for i in every:
            finish(i)

        write_back.wait()
        pl.when(has_after)(forward.wait_send)
        for copy in ahead:
            pl.when(sends_ahead)(copy.wait_send)
        for i in range(NX):
            pl.when(x != i)(backs[i].wait_send)
        for copy in swaps[0] + swaps[1] + swaps[2] + gather_x + gather_y + gather_z + sends:
            copy.wait_send()

    return kernel


def hand_on(attended, grad, attended_out, grad_out):
    attended_out[...] = attended[...]
    grad_out[...] = grad[...]


def body(query_rows, key_rows, value_rows, frame_counts, history, offsets, cotangent):
    tok, feat = query_rows.shape
    tiles = history.shape[0]
    outs = cotangent.shape[1]
    blocks = lax.axis_size("tm")
    nz = blocks // (NX * NY)
    rows = outs // blocks
    half = feat // 2
    clip_rows = tiles * blocks
    total_rows = clip_rows + tok
    lines = tiles * feat // 128
    dma = pltpu.SemaphoreType.DMA
    anywhere = pl.BlockSpec(memory_space=pltpu.HBM)
    vmem = pl.BlockSpec(memory_space=pltpu.VMEM)
    streams = STREAMS
    width = half
    stream_scratch = []
    for _ in streams:
        stream_scratch += [
            pltpu.VMEM((2, 4, nz, rows, width), BF16),
            pltpu.VMEM((2, 4, nz, rows, width), BF16),
            pltpu.VMEM((4, nz, rows, width), F32),
            pltpu.VMEM((3, nz, rows, width), BF16),
            pltpu.VMEM((3, nz, rows, width), BF16),
            pltpu.VMEM((nz - 1, rows, width), BF16),
            pltpu.VMEM((nz - 1, rows, width), BF16),
            dma((2, 4)),
            dma((2, 4)),
            dma((3,)),
            dma((3,)),
            dma((nz - 1,)),
            dma((nz - 1,)),
            pltpu.VMEM((4, nz, rows, width), BF16),
            pltpu.VMEM((4, nz, rows, width), BF16),
            dma((4,)),
            dma((4,)),
            pltpu.VMEM((4, nz, rows, width), F32),
        ]
    results = pl.pallas_call(
        make_kernel(blocks, tok, feat, tiles, outs, streams),
        out_shape=(
            jax.ShapeDtypeStruct((tok, feat), BF16),
            jax.ShapeDtypeStruct((rows, feat), F32),
        ),
        in_specs=[
            pl.BlockSpec(memory_space=pltpu.SMEM),
            anywhere,
            anywhere,
            anywhere,
            vmem,
            vmem,
            anywhere,
        ],
        out_specs=(anywhere, vmem),
        scratch_shapes=[
            pltpu.VMEM((NX, tok, HD), BF16),
            pltpu.VMEM((WINB - 1 + NX, tok, HD), BF16),
            pltpu.VMEM((WINB - 1 + NX, tok, HD), BF16),
            pltpu.VMEM((NX, tok, HD), BF16),
            pltpu.VMEM((total_rows, outs), BF16),
            pltpu.VMEM((NX, NY, nz, rows, total_rows), BF16),
            pltpu.VMEM((total_rows, feat), BF16),
            pltpu.VMEM((blocks, lines, 128), BF16),
            pltpu.VMEM((blocks, lines, 128), F32),
            dma((6,)),
            dma((1,)),
            dma((1,)),
            dma((NX,)),
            dma((NX - 1,)),
            dma((9,)),
            dma((9,)),
            dma((NX,)),
            dma((NX,)),
            dma((6 + nz - 1,)),
            dma((6 + nz - 1,)),
        ]
        + stream_scratch,
        compiler_params=pltpu.CompilerParams(
            collective_id=0, has_side_effects=True, vmem_limit_bytes=60 << 20
        ),
    )(
        frame_counts,
        query_rows,
        key_rows,
        value_rows,
        history,
        offsets,
        cotangent,
    )
    return pl.pallas_call(
        hand_on,
        out_shape=(
            jax.ShapeDtypeStruct((tok, feat), BF16),
            jax.ShapeDtypeStruct((rows, feat), F32),
        ),
        in_specs=[vmem, vmem],
        out_specs=(vmem, vmem),
    )(*results)


def solution(mesh):
    in_specs = (
        P("tm", "head"),
        P("tm", "head"),
        P("tm", "head"),
        P(),
        P("tm", "head"),
        P("tm", None),
        P("tm", None),
    )
    out_specs = (P("tm", "head"), P("tm", "head"))
    return jax.shard_map(body, mesh=mesh, in_specs=in_specs, out_specs=out_specs, check_vma=False)
```

```python
import math

import jax
import jax.numpy as jnp
from jax import lax
from jax.experimental import pallas as pl
from jax.experimental.pallas import tpu as pltpu
from jax.sharding import PartitionSpec as P

HD = 128
TPF = 64
WINB = 4
NX = 4
NY = 4
STREAMS = (0, 1)
MESH = pl.DeviceIdType.MESH
F32 = jnp.float32
BF16 = jnp.bfloat16


def remote(src, dst, send, recv, target):
    return pltpu.make_async_remote_copy(
        src_ref=src,
        dst_ref=dst,
        send_sem=send,
        recv_sem=recv,
        device_id={"tm": target},
        device_id_type=MESH,
    )


def make_kernel(blocks, tok, feat, tiles, outs, streams):
    nz = blocks // (NX * NY)
    half = feat // 2
    halves = (slice(0, half), slice(half, feat))
    heads = feat // HD
    rows = outs // blocks
    plane = outs // NX
    scale = 1.0 / math.sqrt(HD)

    def kernel(
        counts_hbm, query_hbm, key_hbm, value_hbm, history_hbm, offsets_hbm, cot_hbm,
        attended_ref, grad_ref,
        history, offsets, counts, query, keys, values, mixed, cot, cot_t, clip, hist_all, hist_f32,
        local_sem, row_send, row_recv, ahead_send, ahead_recv, kv_send, kv_recv, out_send, out_recv, ag_send, ag_recv,
        *stream_refs,
    ):
        me = lax.axis_index("tm")
        refs = [stream_refs[18 * i : 18 * (i + 1)] for i in range(len(streams))]
        x = lax.rem(me, NX)
        y = lax.rem(me // NX, NY)
        z = me // (NX * NY)

        def at_x(k):
            return me - x + lax.rem(x + k, NX)

        def at_y(k):
            return me + (lax.rem(y + k, NY) - y) * NX

        def at_z(k):
            return me + (lax.rem(z + k, nz) - z) * (NX * NY)

        has_before = me >= NX
        has_after = me + NX < blocks
        peers = [at_x(k) for k in range(1, NX)]
        peers += [at_y(k) for k in range(1, NY)]
        peers += [at_z(k) for k in range(1, nz)]

        def columns(head):
            return pl.ds(pl.multiple_of(head * HD, HD), HD)

        own_head = columns(x)
        last = WINB - 1
        local = [
            pltpu.make_async_copy(cot_hbm, cot, local_sem.at[0]),
            pltpu.make_async_copy(query_hbm.at[:, own_head], query.at[x], local_sem.at[1]),
            pltpu.make_async_copy(key_hbm.at[:, own_head], keys.at[last + x], local_sem.at[2]),
            pltpu.make_async_copy(value_hbm.at[:, own_head], values.at[last + x], local_sem.at[3]),
            pltpu.make_async_copy(history_hbm, history, local_sem.at[4]),
            pltpu.make_async_copy(offsets_hbm, offsets, local_sem.at[6]),
            pltpu.make_async_copy(counts_hbm, counts, local_sem.at[7]),
        ]

        barrier = pltpu.get_barrier_semaphore()
        for peer in peers:
            pl.semaphore_signal(barrier, inc=1, device_id={"tm": peer}, device_id_type=MESH)
        @pl.when(has_before)
        def _():
            for i in range(NX):
                pl.semaphore_signal(
                    barrier, inc=1, device_id={"tm": me - x - NX + i}, device_id_type=MESH
                )

        for copy in local:
            copy.start()
        pl.semaphore_wait(barrier, len(peers) + jnp.where(has_after, NX, 0))

        swaps = []
        for which, (src, dst, first) in enumerate(
            ((key_hbm, keys, last), (value_hbm, values, last), (query_hbm, query, 0))
        ):
            swaps.append(
                [
                    remote(
                        src.at[:, columns(lax.rem(x + k, NX))],
                        dst.at[first + x],
                        kv_send.at[which * (NX - 1) + k - 1],
                        kv_recv.at[which * (NX - 1) + k - 1],
                        at_x(k),
                    )
                    for k in range(1, NX)
                ]
            )
        ahead = [
            remote(
                key_hbm.at[:, i * HD : (i + 1) * HD],
                keys.at[jnp.maximum(x - 1, 0)],
                ahead_send.at[i],
                ahead_recv.at[jnp.maximum(x - 1, 0)],
                lax.rem(me - x + NX + i, blocks),
            )
            for i in range(NX)
        ]
        sends_ahead = has_after & (x > 0)
        forward = remote(
            values.at[WINB : WINB + NX - 1],
            values.at[0 : NX - 1],
            row_send.at[0],
            row_recv.at[0],
            lax.rem(me + NX, blocks),
        )

        def arrive_ahead():
            for i in range(NX - 1):
                remote(
                    key_hbm.at[:, 0:HD],
                    keys.at[i],
                    ahead_send.at[i],
                    ahead_recv.at[i],
                    lax.rem(me + NX, blocks),
                ).wait_recv()

        def gather(first, width, slot, targets):
            block = hist_all.at[pl.ds(first, width)]
            copies = []
            for i, target in enumerate(targets):
                copies.append(
                    remote(block, block, ag_send.at[slot + i], ag_recv.at[slot + i], target)
                )
            return copies

        column = (y * NX + x) * nz
        gather_z = gather(column + z, 1, 6, [at_z(k) for k in range(1, nz)])
        gather_x = gather(column, nz, 0, [at_x(k) for k in range(1, NX)])
        gather_y = gather(y * NX * nz, NX * nz, 3, [at_y(k) for k in range(1, NY)])

        def start(copies):
            for copy in copies:
                copy.start()

        def arrive(copies):
            for copy in copies:
                copy.wait_recv()

        local[4].wait()
        line = history[...].astype(F32)
        hist_all[column + z] = jnp.concatenate(
            [line[t : t + 1, c * 128 : (c + 1) * 128] for t in range(tiles) for c in range(heads)],
            axis=0,
        ).astype(BF16)
        start(gather_z)
        start(swaps[1])

        @pl.when(sends_ahead)
        def _():
            for copy in ahead:
                copy.start()

        start(swaps[0])
        start(swaps[2])

        @pl.when(jnp.logical_not(has_before))
        def _():
            keys[0 : NX - 1] = jnp.zeros((NX - 1, tok, HD), BF16)
            values[0 : NX - 1] = jnp.zeros((NX - 1, tok, HD), BF16)

        def turn(c, _):
            block = cot[:, pl.ds(pl.multiple_of(c * 128, 128), 128)].T
            for e in range(128 // (NX * rows)):
                zy = c * (128 // (NX * rows)) + e
                to_y = lax.rem(lax.rem(zy, NY) + NY - y, NY)
                to_z = lax.rem(zy // NY + nz - z, nz)
                for i in range(NX):
                    first = (e * NX + i) * rows
                    cot_t[lax.rem(i + NX - x, NX), to_y, to_z] = block[first : first + rows]
            return 0

        local[0].wait()
        turns = outs // 128
        lax.fori_loop(0, turns // 2, turn, 0)
        local[3].wait()
        arrive(swaps[1])
        pl.when(has_after)(forward.start)
        arrive(gather_z)
        start(gather_x)
        lax.fori_loop(turns // 2, turns, turn, 0)

        local[6].wait()
        kept = []
        frame = lax.broadcasted_iota(jnp.int32, (1, tok), 1) // TPF
        for slot in range(last + NX):
            source = me - x - last + slot
            count = jnp.where(source >= 0, counts[jnp.maximum(source, 0)], 0)
            kept.append(frame < count)

        clip_rows = tiles * blocks
        local[5].wait()
        tile = jnp.bitwise_and(me - offsets[...], blocks - 1)
        tile = lax.rem(tile, NX * NY) * nz + tile // (NX * NY)
        spread = (
            lax.broadcasted_iota(jnp.int32, (blocks, clip_rows), 1) // tiles
            == lax.broadcasted_iota(jnp.int32, (blocks, clip_rows), 0)
        )
        spread = jnp.where(spread, 1.0, 0.0).astype(BF16)
        source_tile = jnp.dot(
            jnp.broadcast_to(tile.astype(F32).astype(BF16), (16, blocks)),
            spread,
            preferred_element_type=F32,
        )[0:1]
        hist_row = lax.broadcasted_iota(jnp.int32, (clip_rows, clip_rows), 0)
        clip_row = lax.broadcasted_iota(jnp.int32, (clip_rows, clip_rows), 1)
        chosen = (lax.rem(hist_row, blocks).astype(F32) == source_tile) & (
            hist_row // blocks == lax.rem(clip_row, tiles)
        )
        chosen = jnp.where(chosen, 1.0, 0.0).astype(BF16)

        arrive(gather_x)
        start(gather_y)

        def attend(i):
            key_head = keys[i : i + WINB].reshape(WINB * tok, HD)
            value_head = values[i : i + WINB].reshape(WINB * tok, HD)
            scores = lax.dot_general(
                query[i], key_head, (((1,), (1,)), ((), ())), preferred_element_type=F32
            )
            seen = jnp.concatenate(kept[i : i + WINB], axis=1)
            scores = jnp.where(seen, scores * scale, -jnp.inf)
            weights = jnp.exp(scores - jnp.max(scores, axis=1, keepdims=True))
            probs = weights * (1.0 / jnp.sum(weights, axis=1, keepdims=True))
            mixed[i] = jnp.dot(
                probs.astype(BF16), value_head, preferred_element_type=F32
            ).astype(BF16)

        attended = clip.at[clip_rows : clip_rows + tok]
        backs = [
            remote(
                mixed.at[i],
                attended.at[:, own_head],
                out_send.at[i],
                out_recv.at[x],
                me - x + i,
            )
            for i in range(NX)
        ]
        stay = pltpu.make_async_copy(mixed.at[x], attended.at[:, own_head], local_sem.at[1])
        local[1].wait()
        local[2].wait()
        arrive(swaps[0])
        arrive(swaps[2])
        for i in range(NX - 1, -1, -1):
            if i == NX - 2:
                pl.when(has_before)(arrive_ahead)
                pl.when(has_before)(forward.wait_recv)
            attend(i)
            pl.when(x != i)(backs[i].start)
        stay.start()

        arrive(gather_y)
        hist_f32[...] = hist_all[...].astype(F32)
        pieces = []
        for t in range(tiles):
            line = [hist_f32[:, t * heads + c, :] for c in range(heads)]
            pieces.append(jnp.concatenate(line, axis=1))
        hist_rows = jnp.concatenate(pieces, axis=0).astype(BF16)
        clip[0:clip_rows] = lax.dot_general(
            chosen, hist_rows, (((0,), (0,)), ((), ())), preferred_element_type=F32
        ).astype(BF16)
        for k in range(1, NX):
            other = lax.rem(x + k, NX)
            remote(
                mixed.at[0], attended.at[:, columns(other)], out_send.at[0], out_recv.at[other], at_x(k)
            ).wait_recv()
        stay.wait()

        reach = (at_x, at_y)
        sends = []

        def send(src, dst, send_sem, recv_sem, target):
            copy = remote(src, dst, send_sem, recv_sem, target)
            copy.start()
            sends.append(copy)
            return copy

        stage2 = [[None] * 3 for _ in streams]
        stage3 = [[None] * (nz - 1) for _ in streams]
        relays = [[None] * 4 for _ in streams]
        direct = [[[None] * 4 for _ in range(2)] for _ in streams]

        def dot1(i, k):
            left = cot_t[k] if streams[i] == 0 else cot_t[:, k]
            return jnp.dot(
                left.reshape(outs // 4, clip_rows + tok),
                clip[:, halves[i]],
                preferred_element_type=F32,
            ).reshape(4, nz, rows, half)

        up, down = (1, 3), (2, 0)

        def opposite(i):
            s0, r0 = refs[i][13], refs[i][14]
            s0[...] = dot1(i, 2).astype(BF16)
            for j in (1, 2, 3, 0):
                relays[i][j] = send(
                    s0.at[j],
                    r0.at[j],
                    refs[i][15].at[j],
                    refs[i][16].at[j],
                    reach[streams[i]](1 if j in up else 3),
                )

        def pass1(i, side, js):
            s1, r1, s1_sem, r1_sem = refs[i][0], refs[i][1], refs[i][7], refs[i][8]
            for j in js:
                direct[i][side][j] = send(
                    s1.at[side, j],
                    r1.at[side, j],
                    s1_sem.at[side, j],
                    r1_sem.at[side, j],
                    reach[streams[i]](1 if side == 0 else 3),
                )

        def beside(i, side):
            block = dot1(i, 1 if side == 0 else 3)
            through = up if side == 0 else down
            for j in range(4):
                if j in through:
                    refs[i][17][j] = block[j]
                else:
                    refs[i][0][side, j] = block[j].astype(BF16)
            pass1(i, side, down if side == 0 else up)

        def through1(i, side):
            for j in up if side == 0 else down:
                relays[i][j].wait_recv()
                total = refs[i][17][j] + refs[i][14][j].astype(F32)
                refs[i][0][side, j] = total.astype(BF16)
                pass1(i, side, (j,))

        def second(i, j):
            r1, own1, s2, r2 = refs[i][1], refs[i][2], refs[i][3], refs[i][4]
            direct[i][0][j].wait_recv()
            direct[i][1][j].wait_recv()
            total = own1[j] + r1[0, j].astype(F32) + r1[1, j].astype(F32)
            if j == 0:
                own1[0] = total
                return
            s2[j - 1] = total.astype(BF16)
            stage2[i][j - 1] = send(
                s2.at[j - 1],
                r2.at[j - 1],
                refs[i][9].at[j - 1],
                refs[i][10].at[j - 1],
                reach[1 - streams[i]](j),
            )

        def third(i):
            own1, r2, s3, r3 = refs[i][2], refs[i][4], refs[i][5], refs[i][6]
            arrive(stage2[i])
            total = own1[0]
            for k in range(3):
                total += r2[k].astype(F32)
            own1[1, 0] = total[0]
            s3[...] = total[1:].astype(BF16)
            for k in range(1, nz):
                stage3[i][k - 1] = send(
                    s3.at[k - 1],
                    r3.at[k - 1],
                    refs[i][11].at[k - 1],
                    refs[i][12].at[k - 1],
                    at_z(k),
                )

        def finish(i):
            arrive(stage3[i])
            total = refs[i][2][1, 0]
            for k in range(nz - 1):
                total += refs[i][6][k].astype(F32)
            grad_ref[:, halves[i]] = total

        every = range(len(streams))
        for i in every:
            opposite(i)
        for side in range(2):
            for i in every:
                beside(i, side)
        for i in every:
            refs[i][2][...] = dot1(i, 0)
        for side in range(2):
            for i in every:
                through1(i, side)
        write_back = pltpu.make_async_copy(
            attended, attended_ref, local_sem.at[5]
        )
        write_back.start()
        for j in (1, 2, 3, 0):
            for i in every:
                second(i, j)
        for i in every:
            third(i)
        write_back.wait()
        pl.when(has_after)(forward.wait_send)
        for copy in ahead:
            pl.when(sends_ahead)(copy.wait_send)
        for i in range(NX):
            pl.when(x != i)(backs[i].wait_send)
        for copy in swaps[0] + swaps[1] + swaps[2] + gather_x + gather_y + gather_z + sends:
            copy.wait_send()
        for i in every:
            finish(i)

    return kernel


def body(query_rows, key_rows, value_rows, frame_counts, history, offsets, cotangent):
    tok, feat = query_rows.shape
    tiles = history.shape[0]
    outs = cotangent.shape[1]
    blocks = lax.axis_size("tm")
    nz = blocks // (NX * NY)
    rows = outs // blocks
    half = feat // 2
    clip_rows = tiles * blocks
    total_rows = clip_rows + tok
    lines = tiles * feat // 128
    dma = pltpu.SemaphoreType.DMA
    anywhere = pl.BlockSpec(memory_space=pltpu.HBM)
    vmem = pl.BlockSpec(memory_space=pltpu.VMEM)
    streams = STREAMS
    width = half
    stream_scratch = []
    for _ in streams:
        stream_scratch += [
            pltpu.VMEM((2, 4, nz, rows, width), BF16),
            pltpu.VMEM((2, 4, nz, rows, width), BF16),
            pltpu.VMEM((4, nz, rows, width), F32),
            pltpu.VMEM((3, nz, rows, width), BF16),
            pltpu.VMEM((3, nz, rows, width), BF16),
            pltpu.VMEM((nz - 1, rows, width), BF16),
            pltpu.VMEM((nz - 1, rows, width), BF16),
            dma((2, 4)),
            dma((2, 4)),
            dma((3,)),
            dma((3,)),
            dma((nz - 1,)),
            dma((nz - 1,)),
            pltpu.VMEM((4, nz, rows, width), BF16),
            pltpu.VMEM((4, nz, rows, width), BF16),
            dma((4,)),
            dma((4,)),
            pltpu.VMEM((4, nz, rows, width), F32),
        ]
    return pl.pallas_call(
        make_kernel(blocks, tok, feat, tiles, outs, streams),
        out_shape=(pltpu.VMEM((tok, feat), BF16), pltpu.VMEM((rows, feat), F32)),
        in_specs=[anywhere] * 7,
        out_specs=(vmem, vmem),
        scratch_shapes=[
            pltpu.VMEM(history.shape, BF16),
            pltpu.VMEM(offsets.shape, jnp.int32),
            pltpu.SMEM(frame_counts.shape, jnp.int32),
            pltpu.VMEM((NX, tok, HD), BF16),
            pltpu.VMEM((WINB - 1 + NX, tok, HD), BF16),
            pltpu.VMEM((WINB - 1 + NX, tok, HD), BF16),
            pltpu.VMEM((NX, tok, HD), BF16),
            pltpu.VMEM((total_rows, outs), BF16),
            pltpu.VMEM((NX, NY, nz, rows, total_rows), BF16),
            pltpu.VMEM((total_rows, feat), BF16),
            pltpu.VMEM((blocks, lines, 128), BF16),
            pltpu.VMEM((blocks, lines, 128), F32),
            dma((8,)),
            dma((1,)),
            dma((1,)),
            dma((NX,)),
            dma((NX - 1,)),
            dma((9,)),
            dma((9,)),
            dma((NX,)),
            dma((NX,)),
            dma((6 + nz - 1,)),
            dma((6 + nz - 1,)),
        ]
        + stream_scratch,
        compiler_params=pltpu.CompilerParams(
            collective_id=0, has_side_effects=True, vmem_limit_bytes=60 << 20
        ),
    )(
        frame_counts,
        query_rows,
        key_rows,
        value_rows,
        history,
        offsets,
        cotangent,
    )


def solution(mesh):
    in_specs = (
        P("tm", "head"),
        P("tm", "head"),
        P("tm", "head"),
        P(),
        P("tm", "head"),
        P("tm", None),
        P("tm", None),
    )
    out_specs = (P("tm", "head"), P("tm", "head"))
    return jax.shard_map(body, mesh=mesh, in_specs=in_specs, out_specs=out_specs, check_vma=False)
```

```python
import math

import jax
import jax.numpy as jnp
from jax import lax
from jax.experimental import pallas as pl
from jax.experimental.pallas import tpu as pltpu
from jax.sharding import PartitionSpec as P

HD = 128
TPF = 64
WINB = 4
NX = 4
NY = 4
STREAMS = (0, 1)
MESH = pl.DeviceIdType.MESH
F32 = jnp.float32
BF16 = jnp.bfloat16


def remote(src, dst, send, recv, target):
    return pltpu.make_async_remote_copy(
        src_ref=src,
        dst_ref=dst,
        send_sem=send,
        recv_sem=recv,
        device_id={"tm": target},
        device_id_type=MESH,
    )


def make_kernel(blocks, tok, feat, tiles, outs, streams):
    nz = blocks // (NX * NY)
    half = feat // 2
    halves = (slice(0, half), slice(half, feat))
    heads = feat // HD
    rows = outs // blocks
    plane = outs // NX
    scale = 1.0 / math.sqrt(HD)

    def kernel(
        counts_hbm, query_hbm, key_hbm, value_hbm, history_hbm, offsets_hbm, cot_hbm,
        attended_ref, grad_ref,
        history, offsets, counts, query, keys, values, mixed, cot, cot_t, clip, hist_all, hist_f32,
        local_sem, row_send, row_recv, ahead_send, ahead_recv, kv_send, kv_recv, out_send, out_recv, ag_send, ag_recv,
        *stream_refs,
    ):
        me = lax.axis_index("tm")
        refs = [stream_refs[14 * i : 14 * (i + 1)] for i in range(len(streams))]
        x = lax.rem(me, NX)
        y = lax.rem(me // NX, NY)
        z = me // (NX * NY)

        def at_x(k):
            return me - x + lax.rem(x + k, NX)

        def at_y(k):
            return me + (lax.rem(y + k, NY) - y) * NX

        def at_z(k):
            return me + (lax.rem(z + k, nz) - z) * (NX * NY)

        has_before = me >= NX
        has_after = me + NX < blocks
        peers = [at_x(k) for k in range(1, NX)]
        peers += [at_y(k) for k in range(1, NY)]
        peers += [at_z(k) for k in range(1, nz)]

        def columns(head):
            return pl.ds(pl.multiple_of(head * HD, HD), HD)

        own_head = columns(x)
        last = WINB - 1
        local = [
            pltpu.make_async_copy(cot_hbm, cot, local_sem.at[0]),
            pltpu.make_async_copy(query_hbm.at[:, own_head], query.at[x], local_sem.at[1]),
            pltpu.make_async_copy(key_hbm.at[:, own_head], keys.at[last + x], local_sem.at[2]),
            pltpu.make_async_copy(value_hbm.at[:, own_head], values.at[last + x], local_sem.at[3]),
            pltpu.make_async_copy(history_hbm, history, local_sem.at[4]),
            pltpu.make_async_copy(offsets_hbm, offsets, local_sem.at[6]),
            pltpu.make_async_copy(counts_hbm, counts, local_sem.at[7]),
        ]

        barrier = pltpu.get_barrier_semaphore()
        for peer in peers:
            pl.semaphore_signal(barrier, inc=1, device_id={"tm": peer}, device_id_type=MESH)
        @pl.when(has_before)
        def _():
            for i in range(NX):
                pl.semaphore_signal(
                    barrier, inc=1, device_id={"tm": me - x - NX + i}, device_id_type=MESH
                )

        for copy in local:
            copy.start()
        pl.semaphore_wait(barrier, len(peers) + jnp.where(has_after, NX, 0))

        swaps = []
        for which, (src, dst, first) in enumerate(
            ((key_hbm, keys, last), (value_hbm, values, last), (query_hbm, query, 0))
        ):
            swaps.append(
                [
                    remote(
                        src.at[:, columns(lax.rem(x + k, NX))],
                        dst.at[first + x],
                        kv_send.at[which * (NX - 1) + k - 1],
                        kv_recv.at[which * (NX - 1) + k - 1],
                        at_x(k),
                    )
                    for k in (2, 1, 3)
                ]
            )
        ahead = [
            remote(
                key_hbm.at[:, i * HD : (i + 1) * HD],
                keys.at[jnp.maximum(x - 1, 0)],
                ahead_send.at[i],
                ahead_recv.at[jnp.maximum(x - 1, 0)],
                lax.rem(me - x + NX + i, blocks),
            )
            for i in range(NX)
        ]
        sends_ahead = has_after & (x > 0)
        forward = remote(
            values.at[WINB : WINB + NX - 1],
            values.at[0 : NX - 1],
            row_send.at[0],
            row_recv.at[0],
            lax.rem(me + NX, blocks),
        )

        def arrive_ahead():
            for i in range(NX - 1):
                remote(
                    key_hbm.at[:, 0:HD],
                    keys.at[i],
                    ahead_send.at[i],
                    ahead_recv.at[i],
                    lax.rem(me + NX, blocks),
                ).wait_recv()

        def gather(first, width, slot, targets):
            block = hist_all.at[pl.ds(first, width)]
            copies = []
            for i, target in enumerate(targets):
                copies.append(
                    remote(block, block, ag_send.at[slot + i], ag_recv.at[slot + i], target)
                )
            return copies

        column = (y * NX + x) * nz
        gather_z = gather(column + z, 1, 6, [at_z(k) for k in range(1, nz)])
        gather_x = gather(column, nz, 0, [at_x(k) for k in range(1, NX)])
        gather_y = gather(y * NX * nz, NX * nz, 3, [at_y(k) for k in range(1, NY)])

        def start(copies):
            for copy in copies:
                copy.start()

        def arrive(copies):
            for copy in copies:
                copy.wait_recv()

        local[4].wait()
        line = history[...].astype(F32)
        hist_all[column + z] = jnp.concatenate(
            [line[t : t + 1, c * 128 : (c + 1) * 128] for t in range(tiles) for c in range(heads)],
            axis=0,
        ).astype(BF16)
        start(gather_z)
        start(swaps[1])

        @pl.when(sends_ahead)
        def _():
            for copy in ahead:
                copy.start()

        start(swaps[0])
        start(swaps[2])

        @pl.when(jnp.logical_not(has_before))
        def _():
            keys[0 : NX - 1] = jnp.zeros((NX - 1, tok, HD), BF16)
            values[0 : NX - 1] = jnp.zeros((NX - 1, tok, HD), BF16)

        def turn(c, _):
            block = cot[:, pl.ds(pl.multiple_of(c * 128, 128), 128)].T
            for e in range(128 // (NX * rows)):
                zy = c * (128 // (NX * rows)) + e
                to_y = lax.rem(lax.rem(zy, NY) + NY - y, NY)
                to_z = lax.rem(zy // NY + nz - z, nz)
                for i in range(NX):
                    first = (e * NX + i) * rows
                    cot_t[lax.rem(i + NX - x, NX), to_y, to_z] = block[first : first + rows]
            return 0

        local[0].wait()
        turns = outs // 128
        lax.fori_loop(0, turns // 2, turn, 0)
        local[3].wait()
        arrive(swaps[1])
        pl.when(has_after)(forward.start)
        arrive(gather_z)
        start(gather_x)
        lax.fori_loop(turns // 2, turns, turn, 0)

        local[6].wait()
        kept = []
        frame = lax.broadcasted_iota(jnp.int32, (1, tok), 1) // TPF
        for slot in range(last + NX):
            source = me - x - last + slot
            count = jnp.where(source >= 0, counts[jnp.maximum(source, 0)], 0)
            kept.append(frame < count)

        clip_rows = tiles * blocks
        local[5].wait()
        tile = jnp.bitwise_and(me - offsets[...], blocks - 1)
        tile = lax.rem(tile, NX * NY) * nz + tile // (NX * NY)
        spread = (
            lax.broadcasted_iota(jnp.int32, (blocks, clip_rows), 1) // tiles
            == lax.broadcasted_iota(jnp.int32, (blocks, clip_rows), 0)
        )
        spread = jnp.where(spread, 1.0, 0.0).astype(BF16)
        source_tile = jnp.dot(
            jnp.broadcast_to(tile.astype(F32).astype(BF16), (16, blocks)),
            spread,
            preferred_element_type=F32,
        )[0:1]
        hist_row = lax.broadcasted_iota(jnp.int32, (clip_rows, clip_rows), 0)
        clip_row = lax.broadcasted_iota(jnp.int32, (clip_rows, clip_rows), 1)
        chosen = (lax.rem(hist_row, blocks).astype(F32) == source_tile) & (
            hist_row // blocks == lax.rem(clip_row, tiles)
        )
        chosen = jnp.where(chosen, 1.0, 0.0).astype(BF16)

        arrive(gather_x)
        start(gather_y)

        def attend(i):
            key_head = keys[i : i + WINB].reshape(WINB * tok, HD)
            value_head = values[i : i + WINB].reshape(WINB * tok, HD)
            scores = lax.dot_general(
                query[i], key_head, (((1,), (1,)), ((), ())), preferred_element_type=F32
            )
            seen = jnp.concatenate(kept[i : i + WINB], axis=1)
            scores = jnp.where(seen, scores * scale, -jnp.inf)
            weights = jnp.exp(scores - jnp.max(scores, axis=1, keepdims=True))
            probs = weights * (1.0 / jnp.sum(weights, axis=1, keepdims=True))
            mixed[i] = jnp.dot(
                probs.astype(BF16), value_head, preferred_element_type=F32
            ).astype(BF16)

        attended = clip.at[clip_rows : clip_rows + tok]
        backs = [
            remote(
                mixed.at[i],
                attended.at[:, own_head],
                out_send.at[i],
                out_recv.at[x],
                me - x + i,
            )
            for i in range(NX)
        ]
        stay = pltpu.make_async_copy(mixed.at[x], attended.at[:, own_head], local_sem.at[1])
        local[1].wait()
        local[2].wait()
        arrive(swaps[0])
        arrive(swaps[2])
        for i in range(NX - 1, -1, -1):
            if i == NX - 2:
                pl.when(has_before)(arrive_ahead)
                pl.when(has_before)(forward.wait_recv)
            attend(i)
            pl.when(x != i)(backs[i].start)
        stay.start()

        arrive(gather_y)
        hist_f32[...] = hist_all[...].astype(F32)
        pieces = []
        for t in range(tiles):
            line = [hist_f32[:, t * heads + c, :] for c in range(heads)]
            pieces.append(jnp.concatenate(line, axis=1))
        hist_rows = jnp.concatenate(pieces, axis=0).astype(BF16)
        clip[0:clip_rows] = lax.dot_general(
            chosen, hist_rows, (((0,), (0,)), ((), ())), preferred_element_type=F32
        ).astype(BF16)
        for k in range(1, NX):
            other = lax.rem(x + k, NX)
            remote(
                mixed.at[0], attended.at[:, columns(other)], out_send.at[0], out_recv.at[other], at_x(k)
            ).wait_recv()
        stay.wait()

        reach = (at_x, at_y)
        sends = []

        def send(src, dst, send_sem, recv_sem, target):
            copy = remote(src, dst, send_sem, recv_sem, target)
            copy.start()
            sends.append(copy)
            return copy

        stage2 = [[None] * 3 for _ in streams]
        relays = [[None] * 4 for _ in streams]
        direct = [[[None] * 4 for _ in range(2)] for _ in streams]

        def dot1(i, k):
            left = cot_t[k] if streams[i] == 0 else cot_t[:, k]
            return jnp.dot(
                left.reshape(outs // 4, clip_rows + tok),
                clip[:, halves[i]],
                preferred_element_type=F32,
            ).reshape(4, nz, rows, half)

        up, down = (1, 3), (2, 0)

        def opposite(i):
            s0, r0 = refs[i][9], refs[i][10]
            s0[...] = dot1(i, 2).astype(BF16)
            for j in (1, 2, 3, 0):
                relays[i][j] = send(
                    s0.at[j],
                    r0.at[j],
                    refs[i][11].at[j],
                    refs[i][12].at[j],
                    reach[streams[i]](1 if j in up else 3),
                )

        def pass1(i, side, js):
            s1, r1, s1_sem, r1_sem = refs[i][0], refs[i][1], refs[i][5], refs[i][6]
            for j in js:
                direct[i][side][j] = send(
                    s1.at[side, j],
                    r1.at[side, j],
                    s1_sem.at[side, j],
                    r1_sem.at[side, j],
                    reach[streams[i]](1 if side == 0 else 3),
                )

        def beside(i, side):
            block = dot1(i, 1 if side == 0 else 3)
            through = up if side == 0 else down
            for j in range(4):
                if j in through:
                    refs[i][13][j] = block[j]
                else:
                    refs[i][0][side, j] = block[j].astype(BF16)
            pass1(i, side, down if side == 0 else up)

        def through1(i, side):
            for j in up if side == 0 else down:
                relays[i][j].wait_recv()
                total = refs[i][13][j] + refs[i][10][j].astype(F32)
                refs[i][0][side, j] = total.astype(BF16)
                pass1(i, side, (j,))

        def second(i, j):
            r1, own1, s2, r2 = refs[i][1], refs[i][2], refs[i][3], refs[i][4]
            direct[i][0][j].wait_recv()
            direct[i][1][j].wait_recv()
            total = own1[j] + r1[0, j].astype(F32) + r1[1, j].astype(F32)
            if j == 0:
                own1[0] = total
                return
            s2[j - 1] = total.astype(BF16)
            stage2[i][j - 1] = send(
                s2.at[j - 1],
                r2.at[j - 1],
                refs[i][7].at[j - 1],
                refs[i][8].at[j - 1],
                reach[1 - streams[i]](j),
            )

        s3, r3, s3_sem, r3_sem = stream_refs[-4:]

        def third():
            for i in every:
                own1, r2 = refs[i][2], refs[i][4]
                arrive(stage2[i])
                total = own1[0]
                for k in range(3):
                    total += r2[k].astype(F32)
                own1[1, 0] = total[0]
                s3[:, :, halves[i]] = total[1:].astype(BF16)
            return [
                send(s3.at[k], r3.at[k], s3_sem.at[k], r3_sem.at[k], at_z(k + 1))
                for k in range(nz - 1)
            ]

        def finish(i):
            total = refs[i][2][1, 0]
            for k in range(nz - 1):
                total += r3[k, :, halves[i]].astype(F32)
            grad_ref[:, halves[i]] = total

        every = range(len(streams))
        for i in every:
            opposite(i)
        for side in range(2):
            for i in every:
                beside(i, side)
        for i in every:
            refs[i][2][...] = dot1(i, 0)
        for side in range(2):
            for i in every:
                through1(i, side)
        write_back = pltpu.make_async_copy(
            attended, attended_ref, local_sem.at[5]
        )
        write_back.start()
        for j in (1, 2, 3, 0):
            for i in every:
                second(i, j)
        stage3 = third()
        write_back.wait()
        pl.when(has_after)(forward.wait_send)
        for copy in ahead:
            pl.when(sends_ahead)(copy.wait_send)
        for i in range(NX):
            pl.when(x != i)(backs[i].wait_send)
        for copy in swaps[0] + swaps[1] + swaps[2] + gather_x + gather_y + gather_z + sends:
            copy.wait_send()
        arrive(stage3)
        for i in every:
            finish(i)

    return kernel


def body(query_rows, key_rows, value_rows, frame_counts, history, offsets, cotangent):
    tok, feat = query_rows.shape
    tiles = history.shape[0]
    outs = cotangent.shape[1]
    blocks = lax.axis_size("tm")
    nz = blocks // (NX * NY)
    rows = outs // blocks
    half = feat // 2
    clip_rows = tiles * blocks
    total_rows = clip_rows + tok
    lines = tiles * feat // 128
    dma = pltpu.SemaphoreType.DMA
    anywhere = pl.BlockSpec(memory_space=pltpu.HBM)
    vmem = pl.BlockSpec(memory_space=pltpu.VMEM)
    streams = STREAMS
    width = half
    stream_scratch = []
    for _ in streams:
        stream_scratch += [
            pltpu.VMEM((2, 4, nz, rows, width), BF16),
            pltpu.VMEM((2, 4, nz, rows, width), BF16),
            pltpu.VMEM((4, nz, rows, width), F32),
            pltpu.VMEM((3, nz, rows, width), BF16),
            pltpu.VMEM((3, nz, rows, width), BF16),
            dma((2, 4)),
            dma((2, 4)),
            dma((3,)),
            dma((3,)),
            pltpu.VMEM((4, nz, rows, width), BF16),
            pltpu.VMEM((4, nz, rows, width), BF16),
            dma((4,)),
            dma((4,)),
            pltpu.VMEM((4, nz, rows, width), F32),
        ]
    stream_scratch += [
        pltpu.VMEM((nz - 1, rows, feat), BF16),
        pltpu.VMEM((nz - 1, rows, feat), BF16),
        dma((nz - 1,)),
        dma((nz - 1,)),
    ]
    return pl.pallas_call(
        make_kernel(blocks, tok, feat, tiles, outs, streams),
        out_shape=(pltpu.VMEM((tok, feat), BF16), pltpu.VMEM((rows, feat), F32)),
        in_specs=[anywhere] * 7,
        out_specs=(vmem, vmem),
        scratch_shapes=[
            pltpu.VMEM(history.shape, BF16),
            pltpu.VMEM(offsets.shape, jnp.int32),
            pltpu.SMEM(frame_counts.shape, jnp.int32),
            pltpu.VMEM((NX, tok, HD), BF16),
            pltpu.VMEM((WINB - 1 + NX, tok, HD), BF16),
            pltpu.VMEM((WINB - 1 + NX, tok, HD), BF16),
            pltpu.VMEM((NX, tok, HD), BF16),
            pltpu.VMEM((total_rows, outs), BF16),
            pltpu.VMEM((NX, NY, nz, rows, total_rows), BF16),
            pltpu.VMEM((total_rows, feat), BF16),
            pltpu.VMEM((blocks, lines, 128), BF16),
            pltpu.VMEM((blocks, lines, 128), F32),
            dma((8,)),
            dma((1,)),
            dma((1,)),
            dma((NX,)),
            dma((NX - 1,)),
            dma((9,)),
            dma((9,)),
            dma((NX,)),
            dma((NX,)),
            dma((6 + nz - 1,)),
            dma((6 + nz - 1,)),
        ]
        + stream_scratch,
        compiler_params=pltpu.CompilerParams(
            collective_id=0, has_side_effects=True, vmem_limit_bytes=60 << 20
        ),
    )(
        frame_counts,
        query_rows,
        key_rows,
        value_rows,
        history,
        offsets,
        cotangent,
    )


def solution(mesh):
    in_specs = (
        P("tm", "head"),
        P("tm", "head"),
        P("tm", "head"),
        P(),
        P("tm", "head"),
        P("tm", None),
        P("tm", None),
    )
    out_specs = (P("tm", "head"), P("tm", "head"))
    return jax.shard_map(body, mesh=mesh, in_specs=in_specs, out_specs=out_specs, check_vma=False)
```

```python
import math

import jax
import jax.numpy as jnp
from jax import lax
from jax.experimental import pallas as pl
from jax.experimental.pallas import tpu as pltpu
from jax.sharding import PartitionSpec as P

HD = 128
TPF = 64
WINB = 4
NX = 4
NY = 4
STREAMS = (0, 1)
MESH = pl.DeviceIdType.MESH
F32 = jnp.float32
BF16 = jnp.bfloat16


def remote(src, dst, send, recv, target):
    return pltpu.make_async_remote_copy(
        src_ref=src,
        dst_ref=dst,
        send_sem=send,
        recv_sem=recv,
        device_id={"tm": target},
        device_id_type=MESH,
    )


def make_kernel(blocks, tok, feat, tiles, outs, streams):
    nz = blocks // (NX * NY)
    half = feat // 2
    halves = (slice(0, half), slice(half, feat))
    heads = feat // HD
    rows = outs // blocks
    plane = outs // NX
    scale = 1.0 / math.sqrt(HD)

    def kernel(
        counts_hbm, query_hbm, key_hbm, value_hbm, history_hbm, offsets_hbm, cot_hbm,
        attended_ref, grad_ref,
        history, offsets, counts, query, keys, values, mixed, cot, cot_t, clip, hist_all, hist_f32,
        local_sem, row_send, row_recv, ahead_send, ahead_recv, kv_send, kv_recv, out_send, out_recv, ag_send, ag_recv,
        *stream_refs,
    ):
        me = lax.axis_index("tm")
        refs = [stream_refs[14 * i : 14 * (i + 1)] for i in range(len(streams))]
        x = lax.rem(me, NX)
        y = lax.rem(me // NX, NY)
        z = me // (NX * NY)

        def at_x(k):
            return me - x + lax.rem(x + k, NX)

        def at_y(k):
            return me + (lax.rem(y + k, NY) - y) * NX

        def at_z(k):
            return me + (lax.rem(z + k, nz) - z) * (NX * NY)

        has_before = me >= NX
        has_after = me + NX < blocks
        peers = [at_x(k) for k in range(1, NX)]
        peers += [at_y(k) for k in range(1, NY)]
        peers += [at_z(k) for k in range(1, nz)]

        def columns(head):
            return pl.ds(pl.multiple_of(head * HD, HD), HD)

        own_head = columns(x)
        last = WINB - 1
        local = [
            pltpu.make_async_copy(cot_hbm, cot, local_sem.at[0]),
            pltpu.make_async_copy(query_hbm.at[:, own_head], query.at[x], local_sem.at[1]),
            pltpu.make_async_copy(key_hbm.at[:, own_head], keys.at[last + x], local_sem.at[2]),
            pltpu.make_async_copy(value_hbm.at[:, own_head], values.at[last + x], local_sem.at[3]),
            pltpu.make_async_copy(history_hbm, history, local_sem.at[4]),
            pltpu.make_async_copy(offsets_hbm, offsets, local_sem.at[6]),
            pltpu.make_async_copy(counts_hbm, counts, local_sem.at[7]),
        ]

        barrier = pltpu.get_barrier_semaphore()
        for peer in peers:
            pl.semaphore_signal(barrier, inc=1, device_id={"tm": peer}, device_id_type=MESH)
        @pl.when(has_before)
        def _():
            for i in range(NX):
                pl.semaphore_signal(
                    barrier, inc=1, device_id={"tm": me - x - NX + i}, device_id_type=MESH
                )

        for copy in local:
            copy.start()
        pl.semaphore_wait(barrier, len(peers) + jnp.where(has_after, NX, 0))

        swaps = []
        for which, (src, dst, first) in enumerate(
            ((key_hbm, keys, last), (value_hbm, values, last), (query_hbm, query, 0))
        ):
            swaps.append(
                [
                    remote(
                        src.at[:, columns(lax.rem(x + k, NX))],
                        dst.at[first + x],
                        kv_send.at[which * (NX - 1) + k - 1],
                        kv_recv.at[which * (NX - 1) + k - 1],
                        at_x(k),
                    )
                    for k in range(1, NX)
                ]
            )
        ahead = [
            remote(
                key_hbm.at[:, i * HD : (i + 1) * HD],
                keys.at[jnp.maximum(x - 1, 0)],
                ahead_send.at[i],
                ahead_recv.at[jnp.maximum(x - 1, 0)],
                lax.rem(me - x + NX + i, blocks),
            )
            for i in range(NX)
        ]
        sends_ahead = has_after & (x > 0)
        forward = remote(
            values.at[WINB : WINB + NX - 1],
            values.at[0 : NX - 1],
            row_send.at[0],
            row_recv.at[0],
            lax.rem(me + NX, blocks),
        )

        def arrive_ahead():
            for i in range(NX - 1):
                remote(
                    key_hbm.at[:, 0:HD],
                    keys.at[i],
                    ahead_send.at[i],
                    ahead_recv.at[i],
                    lax.rem(me + NX, blocks),
                ).wait_recv()

        def gather(first, width, slot, targets):
            block = hist_all.at[pl.ds(first, width)]
            copies = []
            for i, target in enumerate(targets):
                copies.append(
                    remote(block, block, ag_send.at[slot + i], ag_recv.at[slot + i], target)
                )
            return copies

        column = (y * NX + x) * nz
        gather_z = gather(column + z, 1, 6, [at_z(k) for k in range(1, nz)])
        gather_x = gather(column, nz, 0, [at_x(k) for k in range(1, NX)])
        gather_y = gather(y * NX * nz, NX * nz, 3, [at_y(k) for k in range(1, NY)])

        def start(copies):
            for copy in copies:
                copy.start()

        def arrive(copies):
            for copy in copies:
                copy.wait_recv()

        local[4].wait()
        line = history[...].astype(F32)
        hist_all[column + z] = jnp.concatenate(
            [line[t : t + 1, c * 128 : (c + 1) * 128] for t in range(tiles) for c in range(heads)],
            axis=0,
        ).astype(BF16)
        start(gather_z)
        start(swaps[1])

        @pl.when(sends_ahead)
        def _():
            for copy in ahead:
                copy.start()

        start(swaps[0])
        start(swaps[2])

        @pl.when(jnp.logical_not(has_before))
        def _():
            keys[0 : NX - 1] = jnp.zeros((NX - 1, tok, HD), BF16)
            values[0 : NX - 1] = jnp.zeros((NX - 1, tok, HD), BF16)

        def turn(c, _):
            block = cot[:, pl.ds(pl.multiple_of(c * 128, 128), 128)].T
            for e in range(128 // (NX * rows)):
                zy = c * (128 // (NX * rows)) + e
                to_y = lax.rem(lax.rem(zy, NY) + NY - y, NY)
                to_z = lax.rem(zy // NY + nz - z, nz)
                for i in range(NX):
                    first = (e * NX + i) * rows
                    cot_t[lax.rem(i + NX - x, NX), to_y, to_z] = block[first : first + rows]
            return 0

        local[0].wait()
        turns = outs // 128
        lax.fori_loop(0, turns // 2, turn, 0)
        local[3].wait()
        arrive(swaps[1])
        pl.when(has_after)(forward.start)
        arrive(gather_z)
        start(gather_x)
        lax.fori_loop(turns // 2, turns, turn, 0)

        local[6].wait()
        kept = []
        frame = lax.broadcasted_iota(jnp.int32, (1, tok), 1) // TPF
        for slot in range(last + NX):
            source = me - x - last + slot
            count = jnp.where(source >= 0, counts[jnp.maximum(source, 0)], 0)
            kept.append(frame < count)

        clip_rows = tiles * blocks
        local[5].wait()
        tile = jnp.bitwise_and(me - offsets[...], blocks - 1)
        tile = lax.rem(tile, NX * NY) * nz + tile // (NX * NY)
        spread = (
            lax.broadcasted_iota(jnp.int32, (blocks, clip_rows), 1) // tiles
            == lax.broadcasted_iota(jnp.int32, (blocks, clip_rows), 0)
        )
        spread = jnp.where(spread, 1.0, 0.0).astype(BF16)
        source_tile = jnp.dot(
            jnp.broadcast_to(tile.astype(F32).astype(BF16), (16, blocks)),
            spread,
            preferred_element_type=F32,
        )[0:1]
        hist_row = lax.broadcasted_iota(jnp.int32, (clip_rows, clip_rows), 0)
        clip_row = lax.broadcasted_iota(jnp.int32, (clip_rows, clip_rows), 1)
        chosen = (lax.rem(hist_row, blocks).astype(F32) == source_tile) & (
            hist_row // blocks == lax.rem(clip_row, tiles)
        )
        chosen = jnp.where(chosen, 1.0, 0.0).astype(BF16)

        arrive(gather_x)
        start(gather_y)

        def attend(i):
            key_head = keys[i : i + WINB].reshape(WINB * tok, HD)
            value_head = values[i : i + WINB].reshape(WINB * tok, HD)
            scores = lax.dot_general(
                query[i], key_head, (((1,), (1,)), ((), ())), preferred_element_type=F32
            )
            seen = jnp.concatenate(kept[i : i + WINB], axis=1)
            scores = jnp.where(seen, scores * scale, -jnp.inf)
            weights = jnp.exp(scores - jnp.max(scores, axis=1, keepdims=True))
            probs = weights * (1.0 / jnp.sum(weights, axis=1, keepdims=True))
            mixed[i] = jnp.dot(
                probs.astype(BF16), value_head, preferred_element_type=F32
            ).astype(BF16)

        attended = clip.at[clip_rows : clip_rows + tok]
        backs = [
            remote(
                mixed.at[i],
                attended.at[:, own_head],
                out_send.at[i],
                out_recv.at[x],
                me - x + i,
            )
            for i in range(NX)
        ]
        stay = pltpu.make_async_copy(mixed.at[x], attended.at[:, own_head], local_sem.at[1])
        local[1].wait()
        local[2].wait()
        arrive(swaps[0])
        arrive(swaps[2])
        for i in range(NX - 1, -1, -1):
            if i == NX - 2:
                pl.when(has_before)(arrive_ahead)
                pl.when(has_before)(forward.wait_recv)
            attend(i)
            pl.when(x != i)(backs[i].start)
        stay.start()

        arrive(gather_y)
        hist_f32[...] = hist_all[...].astype(F32)
        pieces = []
        for t in range(tiles):
            line = [hist_f32[:, t * heads + c, :] for c in range(heads)]
            pieces.append(jnp.concatenate(line, axis=1))
        hist_rows = jnp.concatenate(pieces, axis=0).astype(BF16)
        clip[0:clip_rows] = lax.dot_general(
            chosen, hist_rows, (((0,), (0,)), ((), ())), preferred_element_type=F32
        ).astype(BF16)
        for k in range(1, NX):
            other = lax.rem(x + k, NX)
            remote(
                mixed.at[0], attended.at[:, columns(other)], out_send.at[0], out_recv.at[other], at_x(k)
            ).wait_recv()
        stay.wait()

        reach = (at_x, at_y)
        sends = []

        def send(src, dst, send_sem, recv_sem, target):
            copy = remote(src, dst, send_sem, recv_sem, target)
            copy.start()
            sends.append(copy)
            return copy

        stage2 = [[None] * 3 for _ in streams]
        relays = [[None] * 4 for _ in streams]
        direct = [[[None] * 4 for _ in range(2)] for _ in streams]

        def dot1(i, k):
            left = cot_t[k] if streams[i] == 0 else cot_t[:, k]
            return jnp.dot(
                left.reshape(outs // 4, clip_rows + tok),
                clip[:, halves[i]],
                preferred_element_type=F32,
            ).reshape(4, nz, rows, half)

        up, down = (1, 3), (2, 0)

        def opposite(i):
            s0, r0 = refs[i][9], refs[i][10]
            s0[...] = dot1(i, 2).astype(BF16)
            for j in (1, 2, 3, 0):
                relays[i][j] = send(
                    s0.at[j],
                    r0.at[j],
                    refs[i][11].at[j],
                    refs[i][12].at[j],
                    reach[streams[i]](1 if j in up else 3),
                )

        def pass1(i, side, js):
            s1, r1, s1_sem, r1_sem = refs[i][0], refs[i][1], refs[i][5], refs[i][6]
            for j in js:
                direct[i][side][j] = send(
                    s1.at[side, j],
                    r1.at[side, j],
                    s1_sem.at[side, j],
                    r1_sem.at[side, j],
                    reach[streams[i]](1 if side == 0 else 3),
                )

        def beside(i, side):
            block = dot1(i, 1 if side == 0 else 3)
            through = up if side == 0 else down
            for j in range(4):
                if j in through:
                    refs[i][13][j] = block[j]
                else:
                    refs[i][0][side, j] = block[j].astype(BF16)
            pass1(i, side, down if side == 0 else up)

        def through1(i, side):
            for j in up if side == 0 else down:
                relays[i][j].wait_recv()
                total = refs[i][13][j] + refs[i][10][j].astype(F32)
                refs[i][0][side, j] = total.astype(BF16)
                pass1(i, side, (j,))

        def second(i, j):
            r1, own1, s2, r2 = refs[i][1], refs[i][2], refs[i][3], refs[i][4]
            direct[i][0][j].wait_recv()
            direct[i][1][j].wait_recv()
            total = own1[j] + r1[0, j].astype(F32) + r1[1, j].astype(F32)
            if j == 0:
                own1[0] = total
                return
            s2[j - 1] = total.astype(BF16)
            stage2[i][j - 1] = send(
                s2.at[j - 1],
                r2.at[j - 1],
                refs[i][7].at[j - 1],
                refs[i][8].at[j - 1],
                reach[1 - streams[i]](j),
            )

        s3, r3, s3_sem, r3_sem = stream_refs[-4:]

        def third():
            for i in every:
                own1, r2 = refs[i][2], refs[i][4]
                arrive(stage2[i])
                total = own1[0]
                for k in range(3):
                    total += r2[k].astype(F32)
                own1[1, 0] = total[0]
                s3[:, :, halves[i]] = total[1:].astype(BF16)
            return [
                send(s3.at[k], r3.at[k], s3_sem.at[k], r3_sem.at[k], at_z(k + 1))
                for k in range(nz - 1)
            ]

        def finish(i):
            total = refs[i][2][1, 0]
            for k in range(nz - 1):
                total += r3[k, :, halves[i]].astype(F32)
            grad_ref[:, halves[i]] = total

        every = range(len(streams))
        for i in every:
            opposite(i)
        for side in range(2):
            for i in every:
                beside(i, side)
        for i in every:
            refs[i][2][...] = dot1(i, 0)
        for side in range(2):
            for i in every:
                through1(i, side)
        write_back = pltpu.make_async_copy(
            attended, attended_ref, local_sem.at[5]
        )
        write_back.start()
        for j in (1, 2, 3, 0):
            for i in every:
                second(i, j)
        stage3 = third()
        write_back.wait()
        pl.when(has_after)(forward.wait_send)
        for copy in ahead:
            pl.when(sends_ahead)(copy.wait_send)
        for i in range(NX):
            pl.when(x != i)(backs[i].wait_send)
        for copy in swaps[0] + swaps[1] + swaps[2] + gather_x + gather_y + gather_z + sends:
            copy.wait_send()
        arrive(stage3)
        for i in every:
            finish(i)

    return kernel


def body(query_rows, key_rows, value_rows, frame_counts, history, offsets, cotangent):
    tok, feat = query_rows.shape
    tiles = history.shape[0]
    outs = cotangent.shape[1]
    blocks = lax.axis_size("tm")
    nz = blocks // (NX * NY)
    rows = outs // blocks
    half = feat // 2
    clip_rows = tiles * blocks
    total_rows = clip_rows + tok
    lines = tiles * feat // 128
    dma = pltpu.SemaphoreType.DMA
    anywhere = pl.BlockSpec(memory_space=pltpu.HBM)
    vmem = pl.BlockSpec(memory_space=pltpu.VMEM)
    streams = STREAMS
    width = half
    stream_scratch = []
    for _ in streams:
        stream_scratch += [
            pltpu.VMEM((2, 4, nz, rows, width), BF16),
            pltpu.VMEM((2, 4, nz, rows, width), BF16),
            pltpu.VMEM((4, nz, rows, width), F32),
            pltpu.VMEM((3, nz, rows, width), BF16),
            pltpu.VMEM((3, nz, rows, width), BF16),
            dma((2, 4)),
            dma((2, 4)),
            dma((3,)),
            dma((3,)),
            pltpu.VMEM((4, nz, rows, width), BF16),
            pltpu.VMEM((4, nz, rows, width), BF16),
            dma((4,)),
            dma((4,)),
            pltpu.VMEM((4, nz, rows, width), F32),
        ]
    stream_scratch += [
        pltpu.VMEM((nz - 1, rows, feat), BF16),
        pltpu.VMEM((nz - 1, rows, feat), BF16),
        dma((nz - 1,)),
        dma((nz - 1,)),
    ]
    return pl.pallas_call(
        make_kernel(blocks, tok, feat, tiles, outs, streams),
        out_shape=(pltpu.VMEM((tok, feat), BF16), pltpu.VMEM((rows, feat), F32)),
        in_specs=[anywhere] * 7,
        out_specs=(vmem, vmem),
        scratch_shapes=[
            pltpu.VMEM(history.shape, BF16),
            pltpu.VMEM(offsets.shape, jnp.int32),
            pltpu.SMEM(frame_counts.shape, jnp.int32),
            pltpu.VMEM((NX, tok, HD), BF16),
            pltpu.VMEM((WINB - 1 + NX, tok, HD), BF16),
            pltpu.VMEM((WINB - 1 + NX, tok, HD), BF16),
            pltpu.VMEM((NX, tok, HD), BF16),
            pltpu.VMEM((total_rows, outs), BF16),
            pltpu.VMEM((NX, NY, nz, rows, total_rows), BF16),
            pltpu.VMEM((total_rows, feat), BF16),
            pltpu.VMEM((blocks, lines, 128), BF16),
            pltpu.VMEM((blocks, lines, 128), F32),
            dma((8,)),
            dma((1,)),
            dma((1,)),
            dma((NX,)),
            dma((NX - 1,)),
            dma((9,)),
            dma((9,)),
            dma((NX,)),
            dma((NX,)),
            dma((6 + nz - 1,)),
            dma((6 + nz - 1,)),
        ]
        + stream_scratch,
        compiler_params=pltpu.CompilerParams(
            collective_id=0, has_side_effects=True, vmem_limit_bytes=60 << 20
        ),
    )(
        frame_counts,
        query_rows,
        key_rows,
        value_rows,
        history,
        offsets,
        cotangent,
    )


def solution(mesh):
    in_specs = (
        P("tm", "head"),
        P("tm", "head"),
        P("tm", "head"),
        P(),
        P("tm", "head"),
        P("tm", None),
        P("tm", None),
    )
    out_specs = (P("tm", "head"), P("tm", "head"))
    return jax.shard_map(body, mesh=mesh, in_specs=in_specs, out_specs=out_specs, check_vma=False)
```
